256 devices in a mesh: section: 8 (over z), dp: 32 (over y, x, core).
Axes of the slice: x: 4, y: 4, z: 8, core: 2. Of those that a mesh axis runs over, the one named last changes fastest.
Arguments:
- section_inputs: bfloat16 [8, 8192, 896], P('section', 'dp'), may hold values from -44 to 44
- cotangent: bfloat16 [8192, 896], P('dp'), may hold values from -6 to 6
- norm_gain: float32 [8, 896], P('section'), may hold values from 0.25 to 1.75
- quant_gate: bfloat16 [8, 896, 2432], P('section', 'dp'), may hold values from -1 to 1
- quant_up: bfloat16 [8, 896, 2432], P('section', 'dp'), may hold values from -1 to 1
- scales: float32 [8, 2], P('section'), may hold values from 0.04 to 0.08
- down_proj: bfloat16 [8, 2432, 896], P('section'), may hold values from -0.125 to 0.125
- master_gate: float32 [8, 896, 2432], P('section', 'dp'), may hold values from -0.3 to 0.3
- master_up: float32 [8, 896, 2432], P('section', 'dp'), may hold values from -0.3 to 0.3
- moment_gate: float32 [8, 896, 2432], P('section', 'dp'), may hold values from -3 to 3
- moment_up: float32 [8, 896, 2432], P('section', 'dp'), may hold values from -3 to 3
- second_gate: float32 [8, 896, 2432], P('section', 'dp'), may hold values from 0.05 to 1
- second_up: float32 [8, 896, 2432], P('section', 'dp'), may hold values from 0.05 to 1
- next_inputs: bfloat16 [8, 8192, 896], P('section', 'dp'), may hold values from -44 to 44
Outputs:
- input_grads: bfloat16 [8, 8192, 896], P('section', 'dp')
- master_gate_new: float32 [8, 896, 2432], P('section', 'dp')
- master_up_new: float32 [8, 896, 2432], P('section', 'dp')
- moment_gate_new: float32 [8, 896, 2432], P('section', 'dp')
- moment_up_new: float32 [8, 896, 2432], P('section', 'dp')
- second_gate_new: float32 [8, 896, 2432], P('section', 'dp')
- second_up_new: float32 [8, 896, 2432], P('section', 'dp')
- new_scales: float32 [8, 2], P('section')
- next_hidden: bfloat16 [8, 8192, 2432], P('section', 'dp')
The draws below stay inside these ranges and needn't reach their ends.
All inputs are finite; a program needn't handle non-finite values. Where the reference program divides by a largest or mean magnitude, that divisor is 1e-20 or more.
Results may differ from the reference program's by a relative error of at most 0.034.
Values may be sent and summed in bfloat16 or wider, within the bound.
A program may use at most 128 MiB of HBM per device.

```python
import math
import jax
import jax.numpy as jnp
from jax import lax

D = 896
HID = 2432
TOK_DEV = 256
LAYERS = 8
TOKENS = 8192
N_DP = 32


def activation_law(key):
    subkeys = jax.random.split(key, 3)
    token_scale = jnp.exp(jax.random.uniform(subkeys[1], (LAYERS, TOKENS, 1), jnp.float32, 0.0, math.log(10.0)))
    feature_scale = jnp.exp(jax.random.uniform(subkeys[0], (LAYERS, 1, D), jnp.float32, 0.0, math.log(10.0)))
    values = jax.random.truncated_normal(subkeys[2], -4.0, 4.0, (LAYERS, TOKENS, D), jnp.float32)
    return (0.1 * values * feature_scale * token_scale).astype(jnp.bfloat16)


def master_law(key):
    subkeys = jax.random.split(key, 3)
    row_scale = jnp.exp(jax.random.uniform(subkeys[0], (LAYERS, D, 1), jnp.float32, 0.0, math.log(10.0)))
    column_scale = jnp.exp(jax.random.uniform(subkeys[1], (LAYERS, 1, HID), jnp.float32, 0.0, math.log(10.0)))
    rising = 1.0 + 2.0 * jnp.arange(D, dtype=jnp.float32).reshape(1, D, 1) / D
    values = jax.random.truncated_normal(subkeys[2], -4.0, 4.0, (LAYERS, D, HID), jnp.float32)
    return 0.00025 * values * row_scale * column_scale * rising


def draw_section_inputs(key, part):
    return activation_law(jax.random.fold_in(key, 11))


def draw_next_inputs(key, part):
    return activation_law(jax.random.fold_in(key, 12))


def draw_master_gate(key, part):
    return master_law(jax.random.fold_in(key, 13))


def draw_master_up(key, part):
    return master_law(jax.random.fold_in(key, 14))


def block_levels(key, extent, cuts, smallest, high):
    gain = 1.0
    for position, shards_of in cuts:
        draws = jax.random.uniform(jax.random.fold_in(jax.random.fold_in(key, 6), position), (shards_of,), jnp.float32, smallest / len(cuts), high / len(cuts))
        gain = gain * jnp.repeat(jnp.exp(draws), extent[position] // shards_of).reshape((-1,) + (1,) * (len(extent) - 1 - position))
    return gain


def scatter_about(own_key, extent, deviation, limit, cuts=(), kind=jnp.bfloat16):
    values = jax.random.normal(own_key, extent, jnp.float32) * deviation
    if len(cuts) > 0:
        values = block_levels(own_key, extent, cuts, -0.22, 0.18) * values
    return jnp.clip(values, min=-limit, max=limit).astype(kind)


def setup_inputs(seed: int = 0) -> dict:
    arg_keys = jax.random.split(jax.random.key(seed), 15)
    return {
        "section_inputs": draw_section_inputs(jax.random.fold_in(arg_keys[14], 71), 0),
        "cotangent": scatter_about(arg_keys[1], (TOKENS, D), 1.0, 6.0, ((0, 32),)),
        "norm_gain": jnp.clip(1.0 + 0.15 * jax.random.normal(arg_keys[2], (LAYERS, D), jnp.float32), 0.25, 1.75),
        "quant_gate": jnp.clip(jax.random.uniform(arg_keys[3], (LAYERS, D, HID), jnp.float32, -1.0, 1.0) * block_levels(arg_keys[3], (LAYERS, D, HID), ((0, 8), (1, 32)), -0.4, 0.0), -1.0, 1.0).astype(jnp.bfloat16),
        "quant_up": jnp.clip(jax.random.uniform(arg_keys[4], (LAYERS, D, HID), jnp.float32, -1.0, 1.0) * block_levels(arg_keys[4], (LAYERS, D, HID), ((0, 8), (1, 32)), -0.4, 0.0), -1.0, 1.0).astype(jnp.bfloat16),
        "scales": jnp.clip(jnp.exp(math.log(0.08) - 0.6931472 * jax.random.uniform(arg_keys[5], (LAYERS, 2), jnp.float32) ** block_levels(arg_keys[5], (LAYERS, 2), ((0, 8),), -0.2, 0.2)), 0.04, 0.08),
        "down_proj": scatter_about(arg_keys[6], (LAYERS, HID, D), HID ** -0.5, 0.125, ((0, 8),)),
        "master_gate": draw_master_gate(jax.random.fold_in(arg_keys[14], 71), 0),
        "master_up": draw_master_up(jax.random.fold_in(arg_keys[14], 71), 0),
        "moment_gate": scatter_about(arg_keys[9], (LAYERS, D, HID), 0.5, 3.0, ((0, 8), (1, 32)), jnp.float32),
        "moment_up": scatter_about(arg_keys[10], (LAYERS, D, HID), 0.5, 3.0, ((0, 8), (1, 32)), jnp.float32),
        "second_gate": jnp.clip(jnp.exp(math.log(1.0) - 2.9957323 * jax.random.uniform(arg_keys[11], (LAYERS, D, HID), jnp.float32) ** block_levels(arg_keys[11], (LAYERS, D, HID), ((0, 8), (1, 32)), -0.2, 0.2)), 0.05, 1.0),
        "second_up": jnp.clip(jnp.exp(math.log(1.0) - 2.9957323 * jax.random.uniform(arg_keys[12], (LAYERS, D, HID), jnp.float32) ** block_levels(arg_keys[12], (LAYERS, D, HID), ((0, 8), (1, 32)), -0.2, 0.2)), 0.05, 1.0),
        "next_inputs": draw_next_inputs(jax.random.fold_in(arg_keys[14], 71), 0),
    }


beta_one = 0.9
beta_two = 0.95
learn_rate = 0.002
decay_rate = 0.1
adam_steps = 100.0
norm_eps = 1e-06
adam_eps = 1e-08
scale_eps = 1e-06

def normalize(inputs, norm_gain):
    widened = inputs.astype(jnp.float32)
    inverse = lax.rsqrt(lax.optimization_barrier(jnp.mean(widened * widened, axis=-1, keepdims=True)) + norm_eps)
    return (widened, inverse, (widened * inverse * norm_gain).astype(jnp.bfloat16))

def silu_slope(preact):
    sigmoid = jax.nn.sigmoid(preact)
    return (preact * sigmoid, sigmoid * (1.0 + preact * (1.0 - sigmoid)))

def transposed(first_op, second_op):
    return lax.dot_general(first_op, second_op, (((1,), (1,)), ((), ())), preferred_element_type=jnp.float32)

def block_back(widened, inverse, normed, norm_gain, gate_full, up_full, scale_pair, down_full, upstream):
    gate_pre = jnp.dot(normed, gate_full, preferred_element_type=jnp.float32) * scale_pair[0]
    up_pre = jnp.dot(normed, up_full, preferred_element_type=jnp.float32) * scale_pair[1]
    hidden_grad = transposed(upstream, down_full)
    active, slopes = silu_slope(gate_pre)
    gate_grad = (hidden_grad * up_pre * slopes).astype(jnp.bfloat16)
    up_grad = (hidden_grad * active).astype(jnp.bfloat16)
    normed_grad = transposed(gate_grad, gate_full) * scale_pair[0] + transposed(up_grad, up_full) * scale_pair[1]
    gained = norm_gain * normed_grad
    mean_term = lax.optimization_barrier(jnp.mean(widened * gained, axis=-1, keepdims=True))
    result = upstream.astype(jnp.float32) + inverse * gained - widened * (inverse * inverse * inverse) * mean_term
    return (result.astype(jnp.bfloat16), jnp.concatenate([gate_grad, up_grad], axis=1))

def adam_update(master, moment_old, second_old, gradient):
    moment_one = beta_one * moment_old + (1.0 - beta_one) * gradient
    moment_two = beta_two * second_old + (1.0 - beta_two) * gradient * gradient
    unbiased_one = moment_one / (1.0 - beta_one ** adam_steps)
    unbiased_two = moment_two / (1.0 - beta_two ** adam_steps)
    updated = master - learn_rate * (unbiased_one / (jnp.sqrt(unbiased_two) + adam_eps) + decay_rate * master)
    return (updated, moment_one, moment_two)

def partner_sum(normed, grads_both):
    normed_parts = normed.reshape(N_DP, TOK_DEV, D)
    grad_parts = grads_both.reshape(N_DP, TOK_DEV, 2 * HID)

    def add_partner(running, pieces):
        partial_sum = lax.dot_general(pieces[0], pieces[1], (((0,), (0,)), ((), ())), preferred_element_type=jnp.float32).astype(jnp.bfloat16)
        partial_sum = lax.optimization_barrier(partial_sum)
        return (running + partial_sum.astype(jnp.float32), None)
    running, unused = lax.scan(add_partner, jnp.zeros((D, 2 * HID), jnp.float32), (normed_parts, grad_parts))
    return running

def reference(section_inputs, cotangent, norm_gain, quant_gate, quant_up, scales, down_proj, master_gate, master_up, moment_gate, moment_up, second_gate, second_up, next_inputs):
    upstream = cotangent
    collected = []
    for layer_index in range(LAYERS - 1, -1, -1):
        widened, inverse, normed = normalize(section_inputs[layer_index], norm_gain[layer_index])
        upstream, grads_both = block_back(widened, inverse, normed, norm_gain[layer_index], quant_gate[layer_index], quant_up[layer_index], scales[layer_index], down_proj[layer_index], upstream)
        summed = partner_sum(normed, grads_both)
        new_gate, mom_gate, sec_gate = adam_update(master_gate[layer_index], moment_gate[layer_index], second_gate[layer_index], summed[:, :HID])
        new_up, mom_up, sec_up = adam_update(master_up[layer_index], moment_up[layer_index], second_up[layer_index], summed[:, HID:])
        scale_gate = jnp.max(jnp.abs(new_gate)) + scale_eps
        scale_up = jnp.max(jnp.abs(new_up)) + scale_eps
        quant_next_gate = (new_gate / scale_gate).astype(jnp.bfloat16)
        quant_next_up = (new_up / scale_up).astype(jnp.bfloat16)
        unused_one, unused_two, next_normed = normalize(next_inputs[layer_index], norm_gain[layer_index])
        gate_next = jnp.dot(next_normed, quant_next_gate, preferred_element_type=jnp.float32) * scale_gate
        up_next = jnp.dot(next_normed, quant_next_up, preferred_element_type=jnp.float32) * scale_up
        hidden_next = (jax.nn.silu(gate_next) * up_next).astype(jnp.bfloat16)
        collected.insert(0, (upstream, new_gate, new_up, mom_gate, mom_up, sec_gate, sec_up, jnp.stack([scale_gate, scale_up]), hidden_next))
    return (jnp.stack([entry[0] for entry in collected]), jnp.stack([entry[1] for entry in collected]), jnp.stack([entry[2] for entry in collected]), jnp.stack([entry[3] for entry in collected]), jnp.stack([entry[4] for entry in collected]), jnp.stack([entry[5] for entry in collected]), jnp.stack([entry[6] for entry in collected]), jnp.stack([entry[7] for entry in collected]), jnp.stack([entry[8] for entry in collected]))
```

```python
import functools
import jax
import jax.numpy as jnp
from jax import lax
from jax.experimental import pallas as pl
from jax.experimental.pallas import tpu as pltpu
from jax.sharding import PartitionSpec as P

beta_one = 0.9
beta_two = 0.95
learn_rate = 0.002
decay_rate = 0.1
adam_steps = 100.0
norm_eps = 1e-06
adam_eps = 1e-08
scale_eps = 1e-06

RING = 4
CORES = 2
ROWS = 28
PAD = 32
MICRO = 4
F32 = jnp.float32
BF16 = jnp.bfloat16
NT = (((1,), (1,)), ((), ()))
NN = (((1,), (0,)), ((), ()))


def mm(a, b, dims=NN):
    return lax.dot_general(a, b, dims, preferred_element_type=F32)


def tiles(count, step=512):
    return [(i, min(step, count - i)) for i in range(0, count, step)]


def coords():
    dp = lax.axis_index("dp")
    chip = dp // CORES
    return chip // RING, chip % RING, dp % CORES


def dp_index(y, x, core):
    return (y * RING + x) * CORES + core


class Copies:
    def __init__(self, send_sem, recv_sem):
        self.send_sem, self.recv_sem = send_sem, recv_sem
        self.sent = []
        self.slots = {}

    def slot(self, key):
        return self.slots.setdefault(key, len(self.slots))

    def start(self, src, dst, key, device):
        copy = pltpu.make_async_remote_copy(
            src_ref=src,
            dst_ref=dst,
            send_sem=self.send_sem.at[len(self.sent)],
            recv_sem=self.recv_sem.at[self.slot(key)],
            device_id={"dp": device},
            device_id_type=pl.DeviceIdType.MESH,
        )
        copy.start()
        self.sent.append(copy)

    def wait_recv(self, dst, key):
        pltpu.make_async_remote_copy(
            src_ref=dst,
            dst_ref=dst,
            send_sem=self.send_sem.at[0],
            recv_sem=self.recv_sem.at[self.slot(key)],
            device_id={"dp": lax.axis_index("dp")},
            device_id_type=pl.DeviceIdType.MESH,
        ).wait_recv()

    def wait_sends(self):
        for copy in self.sent:
            copy.wait_send()


def plane_barrier(extra=()):
    y, x, core = coords()
    sem = pltpu.get_barrier_semaphore()
    for device in (
        dp_index((y + 1) % RING, x, core),
        dp_index((y + RING - 1) % RING, x, core),
        dp_index(y, (x + 1) % RING, core),
        dp_index(y, (x + RING - 1) % RING, core),
        dp_index(y, x, 1 - core),
    ):
        pl.semaphore_signal(sem, inc=1, device_id={"dp": device}, device_id_type=pl.DeviceIdType.MESH)
    for section in extra:
        pl.semaphore_signal(sem, inc=1, device_id={"section": section}, device_id_type=pl.DeviceIdType.MESH)
    pl.semaphore_wait(sem, 5 + len(extra))


def gather_steps(buf, copies, hidden):
    y, x, core = coords()

    def place(half, first, second):
        if half == 0:
            return (y + second) % RING, (x + first) % RING
        return (y + first) % RING, (x + second) % RING

    def piece(half, first, second, which, owner_core=None):
        py, px = place(half, first, second)
        base = dp_index(py, px, core if owner_core is None else owner_core) * PAD
        start, size = {None: (0, PAD), 0: (0, PAD // 2), 1: (PAD // 2, PAD // 2)}[which]
        start = pl.multiple_of(base + start, PAD // 2)
        return buf.at[pl.ds(start, size), pl.ds(half * hidden, hidden)]

    def send(half, first, second, which, axis, step):
        if axis == 0:
            py, px = place(half, step, 0)
            key = ("ag", half, (first - step) % RING, second, which)
        else:
            py, px = place(half, 0, step)
            key = ("ag", half, first, (second - step) % RING, which)
        ref = piece(half, first, second, which)
        copies.start(ref, ref, key, dp_index(py, px, core))

    def sibling(half, first, second):
        ref = piece(half, first, second, None)
        copies.start(ref, ref, ("sib", half, first, second), dp_index(y, x, 1 - core))

    def arrive(half, first, second):
        for which in (0, 1) if 2 in (first if second == 0 else second,) else (None,):
            copies.wait_recv(piece(half, first, second, which), ("ag", half, first, second, which))

    def spread(half, first):
        send(half, first, 0, None, 1, 1)
        send(half, first, 0, None, 1, -1)

    def on_first(half, first):
        arrive(half, first, 0)
        if first == 3:
            send(half, first, 0, 0, 0, 1)
        if first == 1:
            send(half, first, 0, 1, 0, -1)
        spread(half, first)
        sibling(half, first, 0)

    def on_second(half, first, second):
        arrive(half, first, second)
        if second == 3:
            send(half, first, second, 0, 1, 1)
        if second == 1:
            send(half, first, second, 1, 1, -1)
        sibling(half, first, second)

    def begin(half):
        send(half, 0, 0, None, 0, 1)
        send(half, 0, 0, None, 0, -1)
        spread(half, 0)
        sibling(half, 0, 0)

    steps = []
    for first in (3, 1):
        steps += [functools.partial(on_first, half, first) for half in (0, 1)]
    for second in (3, 1):
        steps += [functools.partial(on_second, half, 0, second) for half in (0, 1)]
    steps += [functools.partial(on_first, half, 2) for half in (0, 1)]
    for first in (3, 1, 2):
        for second in (3, 1):
            steps += [functools.partial(on_second, half, first, second) for half in (0, 1)]
    for first in (0, 3, 1, 2):
        steps += [functools.partial(on_second, half, first, 2) for half in (0, 1)]

    def finish():
        for first in (0, 3, 1, 2):
            for second in (0, 3, 1, 2):
                for half in (0, 1):
                    copies.wait_recv(
                        piece(half, first, second, None, 1 - core), ("sib", half, first, second)
                    )

    return begin, steps, finish


def pad_matrix(spread_ref, features):
    padded = spread_ref.shape[1]
    chunk = 128
    for start in range(0, features, chunk):
        row = lax.broadcasted_iota(jnp.int32, (chunk, padded), 0) + start
        col = lax.broadcasted_iota(jnp.int32, (chunk, padded), 1)
        block, inner = col // PAD, col % PAD
        hit = jnp.logical_and(inner < ROWS, block * ROWS + inner == row)
        spread_ref[pl.ds(start, chunk), :] = jnp.where(hit, 1.0, 0.0).astype(BF16)


def rms(inputs):
    widened = inputs.astype(F32)
    return widened, lax.rsqrt(jnp.mean(widened * widened, axis=-1, keepdims=True) + norm_eps)


def back_kernel(
    own_ref, x_ref, cot_ref, gain_ref, scale_ref, down_ref,
    result_ref, rail_ref,
    weights, down_raw, down_pad, spread, normed_pad, wide_pad, inv_ref, gain_pad,
    slope_gate, slope_up, upstream, outgoing, grads, sides,
    send_sem, recv_sem, wave_send, wave_recv, local_sem,
):
    y, x, core = coords()
    section = lax.axis_index("section")
    sections = lax.axis_size("section")
    tokens, features = x_ref.shape
    hidden = down_ref.shape[0]
    padded = spread.shape[1]
    rail = padded // CORES
    chunk = tokens // MICRO
    copies = Copies(send_sem, recv_sem)
    fetch = pltpu.make_async_copy(down_ref, down_raw, local_sem)
    fetch.start()
    mine = pl.multiple_of(lax.axis_index("dp") * PAD, PAD)
    weights[pl.ds(mine, PAD), :] = own_ref[...]
    plane_barrier(((section + 1) % sections, (section + sections - 1) % sections))
    begin, steps, finish = gather_steps(weights, copies, hidden)
    begin(0)
    begin(1)

    pad_matrix(spread, features)
    steps = list(steps)

    def advance(count):
        for _ in range(min(count, len(steps))):
            steps.pop(0)()

    widened, inverse = rms(x_ref[...])
    gain = gain_ref[...]
    normed = (widened * inverse * gain).astype(BF16)
    inv_ref[...] = inverse
    high = gain.astype(BF16)
    rest = gain - high.astype(F32)
    middle = rest.astype(BF16)
    low = (rest - middle.astype(F32)).astype(BF16)
    one_hot = spread[...]
    gain_pad[...] = mm(high, one_hot) + mm(middle, one_hot) + mm(low, one_hot)
    wide_pad[...] = mm(x_ref[...], one_hot)
    normed_pad[...] = mm(normed, one_hot).astype(BF16)

    @pl.when(section == sections - 1)
    def _():
        upstream[...] = mm(cot_ref[...], one_hot).astype(BF16)

    flat = normed_pad[...].T.reshape(padded // (CORES * PAD), CORES, PAD, tokens)
    even = flat[:, 0].reshape(rail, tokens)
    odd = flat[:, 1].reshape(rail, tokens)
    sides[:, pl.ds(0, tokens)] = jnp.where(core == 0, even, odd)
    sides[:, pl.ds(2 * tokens, tokens)] = jnp.where(core == 0, odd, even)
    other = dp_index(y, x, 1 - core)
    copies.start(
        sides.at[:, pl.ds(2 * tokens, tokens)], sides.at[:, pl.ds(tokens, tokens)], "side", other
    )
    advance(4)
    fetch.wait()
    for start, size in tiles(hidden):
        down_pad[pl.ds(start, size), :] = mm(down_raw[pl.ds(start, size), :], one_hot).astype(BF16)
        advance(2)
    advance(len(steps))
    finish()

    for start, size in tiles(hidden):
        cols = pl.ds(start, size)
        gate = mm(normed_pad[...], weights[:, cols]) * scale_ref[0, 0]
        up = mm(normed_pad[...], weights[:, pl.ds(hidden + start, size)]) * scale_ref[0, 1]
        sigmoid = 1.0 / (1.0 + jnp.exp(-gate))
        slope_gate[:, cols] = up * (sigmoid * (1.0 + gate * (1.0 - sigmoid)))
        slope_up[:, cols] = gate * sigmoid

    def wave_copy(part):
        rows = pl.ds(part * chunk, chunk)
        return pltpu.make_async_remote_copy(
            src_ref=outgoing.at[rows],
            dst_ref=upstream.at[rows],
            send_sem=wave_send.at[part],
            recv_sem=wave_recv.at[part],
            device_id={"section": jnp.maximum(section - 1, 0)},
            device_id_type=pl.DeviceIdType.MESH,
        )

    for part in range(MICRO):
        rows = pl.ds(part * chunk, chunk)

        @pl.when(section < sections - 1)
        def _():
            wave_copy(part).wait_recv()

        above = upstream[rows, :]
        for start, size in tiles(hidden):
            cols = pl.ds(start, size)
            hidden_grad = mm(above, down_pad[cols, :], NT)
            grads[rows, cols] = (hidden_grad * slope_gate[rows, cols]).astype(BF16)
            grads[rows, pl.ds(hidden + start, size)] = (hidden_grad * slope_up[rows, cols]).astype(BF16)
        copies.start(
            grads.at[rows], grads.at[pl.ds(tokens + part * chunk, chunk)], ("grads", part), other
        )
        normed_grad = (
            mm(grads[rows, pl.ds(0, hidden)], weights[:, pl.ds(0, hidden)], NT) * scale_ref[0, 0]
            + mm(grads[rows, pl.ds(hidden, hidden)], weights[:, pl.ds(hidden, hidden)], NT) * scale_ref[0, 1]
        )
        gained = gain_pad[...] * normed_grad
        inverse = inv_ref[rows, :]
        wide = wide_pad[rows, :]
        mean = jnp.sum(wide * gained, axis=-1, keepdims=True) * (1.0 / features)
        outgoing[rows, :] = (
            above.astype(F32) + inverse * gained - wide * (inverse * inverse * inverse) * mean
        ).astype(BF16)

        @pl.when(section > 0)
        def _():
            wave_copy(part).start()

    copies.wait_recv(sides.at[:, pl.ds(tokens, tokens)], "side")
    for part in range(MICRO):
        copies.wait_recv(grads.at[pl.ds(tokens + part * chunk, chunk)], ("grads", part))
    both = sides[:, pl.ds(0, 2 * tokens)]
    for start, size in tiles(2 * hidden):
        cols = pl.ds(start, size)
        rail_ref[:, cols] = mm(both, grads[:, cols]).astype(BF16)
    result_ref[...] = mm(outgoing[...], spread[...], NT).astype(BF16)

    @pl.when(section > 0)
    def _():
        for part in range(MICRO):
            wave_copy(part).wait_send()

    copies.wait_sends()


def adam_update(master, moment_old, second_old, gradient):
    moment_one = beta_one * moment_old + (1.0 - beta_one) * gradient
    moment_two = beta_two * second_old + (1.0 - beta_two) * gradient * gradient
    unbiased_one = moment_one / (1.0 - beta_one**adam_steps)
    unbiased_two = moment_two / (1.0 - beta_two**adam_steps)
    updated = master - learn_rate * (
        unbiased_one / (jnp.sqrt(unbiased_two) + adam_eps) + decay_rate * master
    )
    return (updated, moment_one, moment_two)


def reduce_steps(rail, near, whole, near_last, whole_last, copies, hidden):
    y, x, core = coords()

    def place(half, bulk, other):
        if half == 0:
            return (y + bulk) % RING, (x + other) % RING
        return (y + other) % RING, (x + bulk) % RING

    def block(half, bulk, other, which=None):
        py, px = place(half, bulk, other)
        start, size = {None: (0, PAD), 0: (0, PAD // 2), 1: (PAD // 2, PAD // 2)}[which]
        start = pl.multiple_of((py * RING + px) * PAD + start, PAD // 2)
        return rail.at[pl.ds(start, size), pl.ds(half * hidden, hidden)]

    def send(src, dst, key, half, axis, step):
        py, px = place(half, step, 0) if axis == 0 else place(half, 0, step)
        copies.start(src, dst, key, dp_index(py, px, core))

    def far(half, other):
        for which, step in ((0, 1), (1, -1)):
            send(block(half, 2, other, which), near.at[half, other, which], ("n", half, other, which), half, 0, step)

    def pass_on(half, other):
        for which, step in ((0, 1), (1, -1)):
            copies.wait_recv(near.at[half, other, which], ("n", half, other, which))
            ref = block(half, step, other, which)
            ref[...] = (ref[...].astype(F32) + near[half, other, which].astype(F32)).astype(BF16)
            send(block(half, step, other), whole.at[half, other, which], ("w", half, other, which), half, 0, step)

    def settle(half, other):
        for which in (0, 1):
            copies.wait_recv(whole.at[half, other, which], ("w", half, other, which))
        ref = block(half, 0, other)
        ref[...] = (
            ref[...].astype(F32) + whole[half, other, 0].astype(F32) + whole[half, other, 1].astype(F32)
        ).astype(BF16)

    def far_last(half):
        for which, step in ((0, 1), (1, -1)):
            send(block(half, 0, 2, which), near_last.at[half, which], ("nl", half, which), half, 1, step)

    def pass_last(half):
        for which, step in ((0, 1), (1, -1)):
            copies.wait_recv(near_last.at[half, which], ("nl", half, which))
            ref = block(half, 0, step, which)
            ref[...] = (ref[...].astype(F32) + near_last[half, which].astype(F32)).astype(BF16)
            send(block(half, 0, step), whole_last.at[half, which], ("wl", half, which), half, 1, step)

    def total(half):
        for which in (0, 1):
            copies.wait_recv(whole_last.at[half, which], ("wl", half, which))
        return (
            block(half, 0, 0)[...].astype(F32)
            + whole_last[half, 0].astype(F32)
            + whole_last[half, 1].astype(F32)
        )

    return far, pass_on, settle, far_last, pass_last, total


def update_kernel(
    rail_ref, next_ref, gain_ref, mg_ref, mu_ref, og_ref, ou_ref, sg_ref, su_ref,
    out_ref, nmg_ref, nmu_ref, nog_ref, nou_ref, nsg_ref, nsu_ref, scale_ref,
    weights, rail, near, whole, near_last, whole_last, spread, next_pad, block_ref,
    send_sem, recv_sem, local_sem,
):
    y, x, core = coords()
    hidden = out_ref.shape[1]
    features = next_ref.shape[1]
    copies = Copies(send_sem, recv_sem)
    fetch = pltpu.make_async_copy(rail_ref, rail, local_sem)
    fetch.start()
    plane_barrier()
    fetch.wait()
    far, pass_on, settle, far_last, pass_last, total = reduce_steps(
        rail, near, whole, near_last, whole_last, copies, hidden
    )
    order = (2, 1, 3, 0)
    for other in order:
        far(0, other)
        far(1, other)
    pad_matrix(spread, features)
    widened, inverse = rms(next_ref[...])
    next_normed = (widened * inverse * gain_ref[...]).astype(BF16)
    next_pad[...] = mm(next_normed, spread[...]).astype(BF16)
    for other in order:
        pass_on(0, other)
        pass_on(1, other)
    for other in order:
        settle(0, other)
        settle(1, other)
        if other == 2:
            far_last(0)
            far_last(1)
    pass_last(0)
    pass_last(1)

    begin, steps, finish = gather_steps(weights, copies, hidden)
    mine = pl.multiple_of(lax.axis_index("dp") * PAD, PAD)
    for half, ins, outs in (
        (0, (mg_ref, og_ref, sg_ref), (nmg_ref, nog_ref, nsg_ref)),
        (1, (mu_ref, ou_ref, su_ref), (nmu_ref, nou_ref, nsu_ref)),
    ):
        gradient = total(half)[:ROWS]
        updated, moment, second = adam_update(ins[0][...], ins[1][...], ins[2][...], gradient)
        outs[0][...] = updated
        outs[1][...] = moment
        outs[2][...] = second
        peak = jnp.max(jnp.abs(updated), keepdims=True)
        high = peak.astype(BF16).astype(F32)
        middle = (peak - high).astype(BF16).astype(F32)
        low = peak - high - middle
        tail = lax.broadcasted_iota(jnp.int32, (PAD - ROWS, hidden), 0)
        block_ref[pl.ds(0, ROWS), :] = updated
        block_ref[pl.ds(ROWS, PAD - ROWS), :] = jnp.where(
            tail == 0, high, jnp.where(tail == 1, middle, jnp.where(tail == 2, low, 0.0))
        )
        weights[pl.ds(mine, PAD), pl.ds(half * hidden, hidden)] = block_ref[...].astype(BF16)
        begin(half)
    for step in steps:
        step()
    finish()

    peaks = []
    for half in (0, 1):
        heads = weights[:, pl.ds(half * hidden, 128)].astype(F32)
        heads = heads.reshape(heads.shape[0] // PAD, PAD, 128)[:, PAD - 8 :, :]
        level = lax.broadcasted_iota(jnp.int32, heads.shape, 1)
        found = jnp.sum(jnp.where(level >= 4, heads, 0.0), axis=1)
        peaks.append(jnp.max(found, keepdims=True) + scale_eps)
    lane = lax.broadcasted_iota(jnp.int32, scale_ref.shape, 1)
    scale_ref[...] = jnp.where(lane == 0, peaks[0], peaks[1])
    for start, size in tiles(hidden):
        cols = pl.ds(start, size)
        gate = mm(next_pad[...], weights[:, cols])
        up = mm(next_pad[...], weights[:, pl.ds(hidden + start, size)])
        out_ref[:, cols] = (gate / (1.0 + jnp.exp(-gate)) * up).astype(BF16)
    copies.wait_sends()


VMEM = pl.BlockSpec(memory_space=pltpu.VMEM)
SMEM = pl.BlockSpec(memory_space=pltpu.SMEM)
ANY = pl.BlockSpec(memory_space=pl.ANY)


def shards(
    section_inputs,
    cotangent,
    norm_gain,
    quant_gate,
    quant_up,
    scales,
    down_proj,
    master_gate,
    master_up,
    moment_gate,
    moment_up,
    second_gate,
    second_up,
    next_inputs,
):
    tokens, features = cotangent.shape
    hidden = quant_gate.shape[2]
    partners = lax.axis_size("dp")
    padded = partners * PAD
    rail_rows = padded // CORES
    own = jnp.pad(
        jnp.concatenate([quant_gate[0], quant_up[0]], axis=1), ((0, PAD - ROWS), (0, 0))
    )
    dma = pltpu.SemaphoreType.DMA
    result, rail = pl.pallas_call(
        back_kernel,
        out_shape=(
            jax.ShapeDtypeStruct((tokens, features), BF16),
            jax.ShapeDtypeStruct((rail_rows, 2 * hidden), BF16),
        ),
        in_specs=[VMEM, VMEM, VMEM, VMEM, SMEM, ANY],
        out_specs=(VMEM, VMEM),
        scratch_shapes=[
            pltpu.VMEM((padded, 2 * hidden), BF16),
            pltpu.VMEM((hidden, features), BF16),
            pltpu.VMEM((hidden, padded), BF16),
            pltpu.VMEM((features, padded), BF16),
            pltpu.VMEM((tokens, padded), BF16),
            pltpu.VMEM((tokens, padded), F32),
            pltpu.VMEM((tokens, 1), F32),
            pltpu.VMEM((1, padded), F32),
            pltpu.VMEM((tokens, hidden), F32),
            pltpu.VMEM((tokens, hidden), F32),
            pltpu.VMEM((tokens, padded), BF16),
            pltpu.VMEM((tokens, padded), BF16),
            pltpu.VMEM((2 * tokens, 2 * hidden), BF16),
            pltpu.VMEM((rail_rows, 3 * tokens), BF16),
            dma((80,)),
            dma((80,)),
            dma((MICRO,)),
            dma((MICRO,)),
            dma(()),
        ],
        compiler_params=pltpu.CompilerParams(
            collective_id=0, has_side_effects=True, vmem_limit_bytes=60 * 2**20
        ),
    )(own, section_inputs[0], cotangent, norm_gain, scales, down_proj[0])
    row = jax.ShapeDtypeStruct((ROWS, hidden), F32)
    outs = pl.pallas_call(
        update_kernel,
        out_shape=(jax.ShapeDtypeStruct((tokens, hidden), BF16),)
        + (row,) * 6
        + (jax.ShapeDtypeStruct((1, 2), F32),),
        in_specs=[ANY] + [VMEM] * 8,
        out_specs=(VMEM,) * 8,
        scratch_shapes=[
            pltpu.VMEM((padded, 2 * hidden), BF16),
            pltpu.VMEM((rail_rows, 2 * hidden), BF16),
            pltpu.VMEM((2, RING, 2, PAD // 2, hidden), BF16),
            pltpu.VMEM((2, RING, 2, PAD, hidden), BF16),
            pltpu.VMEM((2, 2, PAD // 2, hidden), BF16),
            pltpu.VMEM((2, 2, PAD, hidden), BF16),
            pltpu.VMEM((features, padded), BF16),
            pltpu.VMEM((tokens, padded), BF16),
            pltpu.VMEM((PAD, hidden), F32),
            dma((128,)),
            dma((128,)),
            dma(()),
        ],
        compiler_params=pltpu.CompilerParams(
            collective_id=1, has_side_effects=True, vmem_limit_bytes=60 * 2**20
        ),
    )(
        rail,
        next_inputs[0],
        norm_gain,
        master_gate[0],
        master_up[0],
        moment_gate[0],
        moment_up[0],
        second_gate[0],
        second_up[0],
    )
    next_hidden, new_gate, new_up, mom_gate, mom_up, sec_gate, sec_up, new_scales = outs
    return (
        result[None],
        new_gate[None],
        new_up[None],
        mom_gate[None],
        mom_up[None],
        sec_gate[None],
        sec_up[None],
        new_scales,
        next_hidden[None],
    )


def solution(mesh):
    placed = (
        P("section", "dp", None),
        P("dp", None),
        P("section", None),
        P("section", "dp", None),
        P("section", "dp", None),
        P("section", None),
        P("section", None, None),
        P("section", "dp", None),
        P("section", "dp", None),
        P("section", "dp", None),
        P("section", "dp", None),
        P("section", "dp", None),
        P("section", "dp", None),
        P("section", "dp", None),
    )
    return jax.shard_map(
        shards,
        mesh=mesh,
        in_specs=placed,
        out_specs=(
            P("section", "dp", None),
            P("section", "dp", None),
            P("section", "dp", None),
            P("section", "dp", None),
            P("section", "dp", None),
            P("section", "dp", None),
            P("section", "dp", None),
            P("section", None),
            P("section", "dp", None),
        ),
        check_vma=False,
    )
```

```python
import functools
import jax
import jax.numpy as jnp
from jax import lax
from jax.experimental import pallas as pl
from jax.experimental.pallas import tpu as pltpu
from jax.sharding import PartitionSpec as P

beta_one = 0.9
beta_two = 0.95
learn_rate = 0.002
decay_rate = 0.1
adam_steps = 100.0
norm_eps = 1e-06
adam_eps = 1e-08
scale_eps = 1e-06

RING = 4
CORES = 2
ROWS = 28
PAD = 32
PARTS = (48, 96, 112)
F32 = jnp.float32
BF16 = jnp.bfloat16
NT = (((1,), (1,)), ((), ()))
NN = (((1,), (0,)), ((), ()))


def mm(a, b, dims=NN):
    return lax.dot_general(a, b, dims, preferred_element_type=F32)


def tiles(count, step=512):
    return [(i, min(step, count - i)) for i in range(0, count, step)]


def coords():
    dp = lax.axis_index("dp")
    chip = dp // CORES
    return chip // RING, chip % RING, dp % CORES


def dp_index(y, x, core):
    return (y * RING + x) * CORES + core


class Copies:
    def __init__(self, send_sem, recv_sem):
        self.send_sem, self.recv_sem = send_sem, recv_sem
        self.sent = []
        self.slots = {}

    def slot(self, key):
        return self.slots.setdefault(key, len(self.slots))

    def start(self, src, dst, key, device):
        copy = pltpu.make_async_remote_copy(
            src_ref=src,
            dst_ref=dst,
            send_sem=self.send_sem.at[len(self.sent)],
            recv_sem=self.recv_sem.at[self.slot(key)],
            device_id={"dp": device},
            device_id_type=pl.DeviceIdType.MESH,
        )
        copy.start()
        self.sent.append(copy)

    def wait_recv(self, dst, key):
        pltpu.make_async_remote_copy(
            src_ref=dst,
            dst_ref=dst,
            send_sem=self.send_sem.at[0],
            recv_sem=self.recv_sem.at[self.slot(key)],
            device_id={"dp": lax.axis_index("dp")},
            device_id_type=pl.DeviceIdType.MESH,
        ).wait_recv()

    def wait_sends(self):
        for copy in self.sent:
            copy.wait_send()


def plane_barrier(extra=()):
    y, x, core = coords()
    sem = pltpu.get_barrier_semaphore()
    for device in (
        dp_index((y + 1) % RING, x, core),
        dp_index((y + RING - 1) % RING, x, core),
        dp_index(y, (x + 1) % RING, core),
        dp_index(y, (x + RING - 1) % RING, core),
        dp_index(y, x, 1 - core),
    ):
        pl.semaphore_signal(sem, inc=1, device_id={"dp": device}, device_id_type=pl.DeviceIdType.MESH)
    for section in extra:
        pl.semaphore_signal(sem, inc=1, device_id={"section": section}, device_id_type=pl.DeviceIdType.MESH)
    pl.semaphore_wait(sem, 5 + len(extra))


def gather_steps(buf, copies, hidden):
    y, x, core = coords()

    def place(half, first, second):
        if half == 0:
            return (y + second) % RING, (x + first) % RING
        return (y + first) % RING, (x + second) % RING

    def piece(half, first, second, which, owner_core=None):
        py, px = place(half, first, second)
        base = dp_index(py, px, core if owner_core is None else owner_core) * PAD
        start, size = {None: (0, PAD), 0: (0, PAD // 2), 1: (PAD // 2, PAD // 2)}[which]
        start = pl.multiple_of(base + start, PAD // 2)
        return buf.at[pl.ds(start, size), pl.ds(half * hidden, hidden)]

    def send(half, first, second, which, axis, step):
        if axis == 0:
            py, px = place(half, step, 0)
            key = ("ag", half, (first - step) % RING, second, which)
        else:
            py, px = place(half, 0, step)
            key = ("ag", half, first, (second - step) % RING, which)
        ref = piece(half, first, second, which)
        copies.start(ref, ref, key, dp_index(py, px, core))

    def sibling(half, first, second):
        ref = piece(half, first, second, None)
        copies.start(ref, ref, ("sib", half, first, second), dp_index(y, x, 1 - core))

    def arrive(half, first, second):
        for which in (0, 1) if 2 in (first if second == 0 else second,) else (None,):
            copies.wait_recv(piece(half, first, second, which), ("ag", half, first, second, which))

    def spread(half, first):
        send(half, first, 0, None, 1, 1)
        send(half, first, 0, None, 1, -1)

    def on_first(half, first):
        arrive(half, first, 0)
        if first == 3:
            send(half, first, 0, 0, 0, 1)
        if first == 1:
            send(half, first, 0, 1, 0, -1)
        spread(half, first)
        sibling(half, first, 0)

    def on_second(half, first, second):
        arrive(half, first, second)
        if second == 3:
            send(half, first, second, 0, 1, 1)
        if second == 1:
            send(half, first, second, 1, 1, -1)
        sibling(half, first, second)

    def begin(half):
        send(half, 0, 0, None, 0, 1)
        send(half, 0, 0, None, 0, -1)
        spread(half, 0)
        sibling(half, 0, 0)

    def both(step, *key):
        return [functools.partial(step, half, *key) for half in (0, 1)]

    rounds = (
        both(on_first, 3) + both(on_first, 1),
        both(on_second, 0, 3) + both(on_second, 0, 1) + both(on_first, 2),
        both(on_second, 0, 2),
        both(on_second, 3, 3) + both(on_second, 3, 1) + both(on_second, 1, 3) + both(on_second, 1, 1),
        both(on_second, 3, 2) + both(on_second, 1, 2),
        both(on_second, 2, 3) + both(on_second, 2, 1),
        both(on_second, 2, 2),
    )

    def from_sibling(half, first, second):
        copies.wait_recv(piece(half, first, second, None, 1 - core), ("sib", half, first, second))

    return begin, rounds, from_sibling


def pad_matrix(ref, padded_axis):
    chunk = 128
    for start in range(0, ref.shape[0], chunk):
        shape = (chunk, ref.shape[1])
        ids = [lax.broadcasted_iota(jnp.int32, shape, axis) for axis in (0, 1)]
        ids[0] = ids[0] + start
        plain, number = ids[1 - padded_axis], ids[padded_axis]
        block, inner = number // PAD, number % PAD
        hit = jnp.logical_and(inner < ROWS, block * ROWS + inner == plain)
        ref[pl.ds(start, chunk), :] = jnp.where(hit, 1.0, 0.0).astype(BF16)


def rms(inputs):
    widened = inputs.astype(F32)
    return widened, lax.rsqrt(jnp.mean(widened * widened, axis=-1, keepdims=True) + norm_eps)


def back_kernel(
    own_ref, x_ref, cot_ref, gain_ref, scale_ref, down_ref,
    outgoing, rail_ref,
    weights, turned, down_raw, down_turned, spread, gather, normed_pad, wide_pad, inv_ref, gain_pad,
    slope_gate, slope_up, slope_sum, partial, upstream, grads, sides,
    send_sem, recv_sem, wave_send, wave_recv, local_sem,
):
    y, x, core = coords()
    section = lax.axis_index("section")
    sections = lax.axis_size("section")
    last = sections - 1
    tokens, features = x_ref.shape
    hidden = down_ref.shape[0]
    padded = gather.shape[0]
    rail = padded // CORES
    width = padded // RING
    copies = Copies(send_sem, recv_sem)
    fetch = pltpu.make_async_copy(down_ref, down_raw, local_sem)
    fetch.start()
    mine = pl.multiple_of(lax.axis_index("dp") * PAD, PAD)
    weights[pl.ds(mine, PAD), :] = own_ref[...]
    plane_barrier(((section + 1) % sections, (section + sections - 1) % sections))
    begin, rounds, from_sibling = gather_steps(weights, copies, hidden)
    begin(0)
    begin(1)

    pad_matrix(spread, 1)
    one_hot = spread[...]
    widened, inverse = rms(x_ref[...])
    gain = gain_ref[...]
    normed = (widened * inverse * gain).astype(BF16)
    inv_ref[...] = inverse
    high = gain.astype(BF16)
    rest = gain - high.astype(F32)
    middle = rest.astype(BF16)
    low = (rest - middle.astype(F32)).astype(BF16)
    gain_pad[...] = mm(high, one_hot) + mm(middle, one_hot) + mm(low, one_hot)
    wide_pad[...] = mm(x_ref[...], one_hot)
    normed_pad[...] = mm(normed, one_hot).astype(BF16)

    flat = normed_pad[...].T.reshape(padded // (CORES * PAD), CORES, PAD, tokens)
    even = flat[:, 0].reshape(rail, tokens)
    odd = flat[:, 1].reshape(rail, tokens)
    sides[:, pl.ds(0, tokens)] = jnp.where(core == 0, even, odd)
    sides[:, pl.ds(2 * tokens, tokens)] = jnp.where(core == 0, odd, even)
    other = dp_index(y, x, 1 - core)
    copies.start(
        sides.at[:, pl.ds(2 * tokens, tokens)], sides.at[:, pl.ds(tokens, tokens)], "side", other
    )

    def down_piece(start, size):
        down_turned[:, pl.ds(start, size)] = mm(
            gather[...], down_raw[pl.ds(start, size), :], NT
        ).astype(BF16)

    def weight_rows(half, step):
        for i in range(RING):
            from_sibling(half, *((i, step) if half == 0 else (step, i)))
        rows = pl.ds(pl.multiple_of(((y + step) % RING) * width, width), width)
        target = (slope_gate, slope_up)[half]
        left = normed_pad[:, rows]
        for start, size in tiles(hidden):
            here = weights[rows, pl.ds(half * hidden + start, size)]
            turned[pl.ds(half * hidden + start, size), rows] = here.T
            product = mm(left, here)
            cols = pl.ds(start, size)
            target[:, cols] = product if step == 0 else target[:, cols] + product

    downs = [functools.partial(down_piece, *piece) for piece in tiles(hidden, 256)]

    def run(items):
        for item in items:
            item()
            if downs:
                downs.pop(0)()

    run_plain = lambda items: [item() for item in items]
    run_plain(rounds[0])
    pad_matrix(gather, 0)
    fetch.wait()

    @pl.when(section == last)
    def _():
        upstream[...] = mm(cot_ref[...], one_hot).astype(BF16)

    run(rounds[1])
    run(rounds[2])
    weight_rows(0, 0)
    weight_rows(1, 0)
    run(rounds[3])
    while downs:
        downs.pop(0)()
    run(rounds[4])
    weight_rows(1, 3)
    run(rounds[5])
    weight_rows(1, 1)
    run(rounds[6])
    weight_rows(0, 3)
    weight_rows(0, 1)
    weight_rows(0, 2)
    weight_rows(1, 2)

    parts = []
    for size in PARTS:
        parts.append((sum(PARTS[: len(parts)]), size))

    def slopes(first, count):
        rows = pl.ds(first, count)
        for start, size in tiles(hidden):
            cols = pl.ds(start, size)
            gate = slope_gate[rows, cols] * scale_ref[0, 0]
            up = slope_up[rows, cols] * scale_ref[0, 1]
            sigmoid = 1.0 / (1.0 + jnp.exp(-gate))
            by_gate = up * (sigmoid * (1.0 + gate * (1.0 - sigmoid)))
            by_up = gate * sigmoid
            slope_gate[rows, cols] = by_gate
            slope_up[rows, cols] = by_up
            slope_sum[rows, cols] = by_gate * gate + by_up * up

    slopes(*parts[0])

    @pl.when(section < last)
    def _():
        slopes(parts[1][0], tokens - parts[1][0])

    def wave_copy(part, piece):
        rows, cols = pl.ds(*parts[part]), pl.ds(piece * width, width)
        return pltpu.make_async_remote_copy(
            src_ref=outgoing.at[rows, cols],
            dst_ref=upstream.at[rows, cols],
            send_sem=wave_send.at[part * RING + piece],
            recv_sem=wave_recv.at[part * RING + piece],
            device_id={"section": jnp.maximum(section - 1, 0)},
            device_id_type=pl.DeviceIdType.MESH,
        )

    for part, (first, count) in enumerate(parts):
        rows = pl.ds(first, count)
        if part > 0:

            @pl.when(section == last)
            def _():
                slopes(first, count)

        sums = jnp.zeros((count, 128), F32)
        for piece in range(RING):
            span = pl.ds(piece * width, width)

            @pl.when(section < last)
            def _():
                wave_copy(part, piece).wait_recv()

            left = upstream[rows, span]
            for start, size in tiles(hidden):
                cols = pl.ds(start, size)
                product = mm(left, down_turned[span, cols])
                if piece > 0:
                    product = product + partial[pl.ds(0, count), cols]
                if piece < RING - 1:
                    partial[pl.ds(0, count), cols] = product
                    continue
                grads[rows, cols] = (product * slope_gate[rows, cols]).astype(BF16)
                grads[rows, pl.ds(hidden + start, size)] = (product * slope_up[rows, cols]).astype(BF16)
                product = product * slope_sum[rows, cols]
                for lane in range(0, size, 128):
                    sums = sums + product[:, lane : lane + 128]
        copies.start(grads.at[rows], grads.at[pl.ds(tokens + first, count)], ("grads", part), other)
        inverse = inv_ref[rows, :]
        mean = jnp.sum(sums, axis=-1, keepdims=True) * (inverse * inverse / features)
        for piece in range(RING):
            span = pl.ds(piece * width, width)
            normed_grad = (
                mm(grads[rows, pl.ds(0, hidden)], turned[pl.ds(0, hidden), span]) * scale_ref[0, 0]
                + mm(grads[rows, pl.ds(hidden, hidden)], turned[pl.ds(hidden, hidden), span])
                * scale_ref[0, 1]
            )
            outgoing[rows, span] = (
                upstream[rows, span].astype(F32)
                + inverse * (gain_pad[:, span] * normed_grad)
                - wide_pad[rows, span] * mean
            ).astype(BF16)

            @pl.when(section > 0)
            def _():
                wave_copy(part, piece).start()

    copies.wait_recv(sides.at[:, pl.ds(tokens, tokens)], "side")
    for part, (first, count) in enumerate(parts):
        copies.wait_recv(grads.at[pl.ds(tokens + first, count)], ("grads", part))
    both = sides[:, pl.ds(0, 2 * tokens)]
    for start, size in tiles(2 * hidden):
        cols = pl.ds(start, size)
        rail_ref[:, cols] = mm(both, grads[:, cols]).astype(BF16)

    @pl.when(section > 0)
    def _():
        for part in range(len(parts)):
            for piece in range(RING):
                wave_copy(part, piece).wait_send()

    copies.wait_sends()


def adam_update(master, moment_old, second_old, gradient):
    moment_one = beta_one * moment_old + (1.0 - beta_one) * gradient
    moment_two = beta_two * second_old + (1.0 - beta_two) * gradient * gradient
    unbiased_one = moment_one / (1.0 - beta_one**adam_steps)
    unbiased_two = moment_two / (1.0 - beta_two**adam_steps)
    updated = master - learn_rate * (
        unbiased_one / (jnp.sqrt(unbiased_two) + adam_eps) + decay_rate * master
    )
    return (updated, moment_one, moment_two)


def reduce_steps(rail, near, whole, near_last, whole_last, copies, hidden):
    y, x, core = coords()

    def place(half, bulk, other):
        if half == 0:
            return (y + bulk) % RING, (x + other) % RING
        return (y + other) % RING, (x + bulk) % RING

    def block(half, bulk, other, which=None):
        py, px = place(half, bulk, other)
        start, size = {None: (0, PAD), 0: (0, PAD // 2), 1: (PAD // 2, PAD // 2)}[which]
        start = pl.multiple_of((py * RING + px) * PAD + start, PAD // 2)
        return rail.at[pl.ds(start, size), pl.ds(half * hidden, hidden)]

    def send(src, dst, key, half, axis, step):
        py, px = place(half, step, 0) if axis == 0 else place(half, 0, step)
        copies.start(src, dst, key, dp_index(py, px, core))

    def far(half, other):
        for which, step in ((0, 1), (1, -1)):
            send(block(half, 2, other, which), near.at[half, other, which], ("n", half, other, which), half, 0, step)

    def pass_on(half, other):
        for which, step in ((0, 1), (1, -1)):
            copies.wait_recv(near.at[half, other, which], ("n", half, other, which))
            ref = block(half, step, other, which)
            ref[...] = (ref[...].astype(F32) + near[half, other, which].astype(F32)).astype(BF16)
            send(block(half, step, other), whole.at[half, other, which], ("w", half, other, which), half, 0, step)

    def settle(half, other):
        for which in (0, 1):
            copies.wait_recv(whole.at[half, other, which], ("w", half, other, which))
        ref = block(half, 0, other)
        ref[...] = (
            ref[...].astype(F32) + whole[half, other, 0].astype(F32) + whole[half, other, 1].astype(F32)
        ).astype(BF16)

    def far_last(half):
        for which, step in ((0, 1), (1, -1)):
            send(block(half, 0, 2, which), near_last.at[half, which], ("nl", half, which), half, 1, step)

    def pass_last(half):
        for which, step in ((0, 1), (1, -1)):
            copies.wait_recv(near_last.at[half, which], ("nl", half, which))
            ref = block(half, 0, step, which)
            ref[...] = (ref[...].astype(F32) + near_last[half, which].astype(F32)).astype(BF16)
            send(block(half, 0, step), whole_last.at[half, which], ("wl", half, which), half, 1, step)

    def total(half):
        for which in (0, 1):
            copies.wait_recv(whole_last.at[half, which], ("wl", half, which))
        return (
            block(half, 0, 0)[...].astype(F32)
            + whole_last[half, 0].astype(F32)
            + whole_last[half, 1].astype(F32)
        )

    return far, pass_on, settle, far_last, pass_last, total


def update_kernel(
    rail_ref, back_ref, next_ref, gain_ref, mg_ref, mu_ref, og_ref, ou_ref, sg_ref, su_ref,
    result_ref, out_ref, nmg_ref, nmu_ref, nog_ref, nou_ref, nsg_ref, nsu_ref, scale_ref,
    weights, rail, near, whole, near_last, whole_last, spread, gather, next_pad, block_ref, flat_ref,
    send_sem, recv_sem, local_sem,
):
    y, x, core = coords()
    hidden = out_ref.shape[1]
    features = next_ref.shape[1]
    copies = Copies(send_sem, recv_sem)
    fetch = pltpu.make_async_copy(rail_ref, rail, local_sem)
    fetch.start()
    plane_barrier()
    fetch.wait()
    far, pass_on, settle, far_last, pass_last, total = reduce_steps(
        rail, near, whole, near_last, whole_last, copies, hidden
    )
    order = (2, 1, 3, 0)
    for other in order:
        far(0, other)
        far(1, other)
    pad_matrix(spread, 1)
    widened, inverse = rms(next_ref[...])
    next_normed = (widened * inverse * gain_ref[...]).astype(BF16)
    next_pad[...] = mm(next_normed, spread[...]).astype(BF16)
    pad_matrix(gather, 0)
    result_ref[...] = mm(back_ref[...], gather[...]).astype(BF16)
    for other in order:
        pass_on(0, other)
        pass_on(1, other)
    for other in order:
        settle(0, other)
        settle(1, other)
        if other == 2:
            far_last(0)
            far_last(1)
    pass_last(0)
    pass_last(1)

    begin, rounds, from_sibling = gather_steps(weights, copies, hidden)
    lanes = flat_ref.shape[1]
    lines = hidden // lanes
    mine = pl.multiple_of(lax.axis_index("dp") * PAD, PAD)
    for half, ins, outs in (
        (0, (mg_ref, og_ref, sg_ref), (nmg_ref, nog_ref, nsg_ref)),
        (1, (mu_ref, ou_ref, su_ref), (nmu_ref, nou_ref, nsu_ref)),
    ):
        gradient = total(half)
        for line in range(lines):
            flat_ref[pl.ds(line, ROWS, stride=lines), :] = gradient[:ROWS, line * lanes : (line + 1) * lanes]
        gradient = flat_ref[...]
        updated, moment, second = adam_update(ins[0][...], ins[1][...], ins[2][...], gradient)
        outs[0][...] = updated
        outs[1][...] = moment
        outs[2][...] = second
        peak = jnp.max(jnp.abs(updated), keepdims=True)
        high = peak.astype(BF16).astype(F32)
        middle = (peak - high).astype(BF16).astype(F32)
        low = peak - high - middle
        tail = lax.broadcasted_iota(jnp.int32, (PAD - ROWS, hidden), 0)
        for line in range(lines):
            block_ref[pl.ds(0, ROWS), pl.ds(line * lanes, lanes)] = outs[0][pl.ds(line, ROWS, stride=lines), :]
        block_ref[pl.ds(ROWS, PAD - ROWS), :] = jnp.where(
            tail == 0, high, jnp.where(tail == 1, middle, jnp.where(tail == 2, low, 0.0))
        )
        weights[pl.ds(mine, PAD), pl.ds(half * hidden, hidden)] = block_ref[...].astype(BF16)
        begin(half)
    for group in rounds:
        for step in group:
            step()
    for first in range(RING):
        for second in range(RING):
            from_sibling(0, first, second)
            from_sibling(1, first, second)

    peaks = []
    for half in (0, 1):
        heads = weights[:, pl.ds(half * hidden, 128)].astype(F32)
        heads = heads.reshape(heads.shape[0] // PAD, PAD, 128)[:, PAD - 8 :, :]
        level = lax.broadcasted_iota(jnp.int32, heads.shape, 1)
        found = jnp.sum(jnp.where(level >= 4, heads, 0.0), axis=1)
        peaks.append(jnp.max(found, keepdims=True) + scale_eps)
    lane = lax.broadcasted_iota(jnp.int32, scale_ref.shape, 1)
    scale_ref[...] = jnp.where(lane == 0, peaks[0], peaks[1])
    for start, size in tiles(hidden):
        cols = pl.ds(start, size)
        gate = mm(next_pad[...], weights[:, cols])
        up = mm(next_pad[...], weights[:, pl.ds(hidden + start, size)])
        out_ref[:, cols] = (gate / (1.0 + jnp.exp(-gate)) * up).astype(BF16)
    copies.wait_sends()


VMEM = pl.BlockSpec(memory_space=pltpu.VMEM)
SMEM = pl.BlockSpec(memory_space=pltpu.SMEM)
ANY = pl.BlockSpec(memory_space=pl.ANY)


def shards(
    section_inputs,
    cotangent,
    norm_gain,
    quant_gate,
    quant_up,
    scales,
    down_proj,
    master_gate,
    master_up,
    moment_gate,
    moment_up,
    second_gate,
    second_up,
    next_inputs,
):
    tokens, features = cotangent.shape
    hidden = quant_gate.shape[2]
    partners = lax.axis_size("dp")
    padded = partners * PAD
    rail_rows = padded // CORES
    own = jnp.pad(
        jnp.concatenate([quant_gate[0], quant_up[0]], axis=1), ((0, PAD - ROWS), (0, 0))
    )
    dma = pltpu.SemaphoreType.DMA
    back, rail = pl.pallas_call(
        back_kernel,
        out_shape=(
            jax.ShapeDtypeStruct((tokens, padded), BF16),
            jax.ShapeDtypeStruct((rail_rows, 2 * hidden), BF16),
        ),
        in_specs=[VMEM, VMEM, VMEM, VMEM, SMEM, ANY],
        out_specs=(VMEM, VMEM),
        scratch_shapes=[
            pltpu.VMEM((padded, 2 * hidden), BF16),
            pltpu.VMEM((2 * hidden, padded), BF16),
            pltpu.VMEM((hidden, features), BF16),
            pltpu.VMEM((padded, hidden), BF16),
            pltpu.VMEM((features, padded), BF16),
            pltpu.VMEM((padded, features), BF16),
            pltpu.VMEM((tokens, padded), BF16),
            pltpu.VMEM((tokens, padded), F32),
            pltpu.VMEM((tokens, 1), F32),
            pltpu.VMEM((1, padded), F32),
            pltpu.VMEM((tokens, hidden), F32),
            pltpu.VMEM((tokens, hidden), F32),
            pltpu.VMEM((tokens, hidden), F32),
            pltpu.VMEM((max(PARTS), hidden), F32),
            pltpu.VMEM((tokens, padded), BF16),
            pltpu.VMEM((2 * tokens, 2 * hidden), BF16),
            pltpu.VMEM((rail_rows, 3 * tokens), BF16),
            dma((80,)),
            dma((80,)),
            dma((len(PARTS) * RING,)),
            dma((len(PARTS) * RING,)),
            dma(()),
        ],
        compiler_params=pltpu.CompilerParams(
            collective_id=0, has_side_effects=True, vmem_limit_bytes=60 * 2**20
        ),
    )(own, section_inputs[0], cotangent, norm_gain, scales, down_proj[0])
    lanes = 128
    row = jax.ShapeDtypeStruct((ROWS * hidden // lanes, lanes), F32)
    flat = [
        value.reshape(row.shape)
        for value in (master_gate, master_up, moment_gate, moment_up, second_gate, second_up)
    ]
    outs = pl.pallas_call(
        update_kernel,
        out_shape=(
            jax.ShapeDtypeStruct((tokens, features), BF16),
            jax.ShapeDtypeStruct((tokens, hidden), BF16),
        )
        + (row,) * 6
        + (jax.ShapeDtypeStruct((1, 2), F32),),
        in_specs=[ANY] + [VMEM] * 9,
        out_specs=(VMEM,) * 9,
        scratch_shapes=[
            pltpu.VMEM((padded, 2 * hidden), BF16),
            pltpu.VMEM((rail_rows, 2 * hidden), BF16),
            pltpu.VMEM((2, RING, 2, PAD // 2, hidden), BF16),
            pltpu.VMEM((2, RING, 2, PAD, hidden), BF16),
            pltpu.VMEM((2, 2, PAD // 2, hidden), BF16),
            pltpu.VMEM((2, 2, PAD, hidden), BF16),
            pltpu.VMEM((features, padded), BF16),
            pltpu.VMEM((padded, features), BF16),
            pltpu.VMEM((tokens, padded), BF16),
            pltpu.VMEM((PAD, hidden), F32),
            pltpu.VMEM(row.shape, F32),
            dma((128,)),
            dma((128,)),
            dma(()),
        ],
        compiler_params=pltpu.CompilerParams(
            collective_id=1, has_side_effects=True, vmem_limit_bytes=60 * 2**20
        ),
    )(rail, back, next_inputs[0], norm_gain, *flat)
    result, next_hidden = outs[:2]
    return (
        (result[None],)
        + tuple(value.reshape(master_gate.shape) for value in outs[2:8])
        + (outs[8], next_hidden[None])
    )


def solution(mesh):
    placed = (
        P("section", "dp", None),
        P("dp", None),
        P("section", None),
        P("section", "dp", None),
        P("section", "dp", None),
        P("section", None),
        P("section", None, None),
        P("section", "dp", None),
        P("section", "dp", None),
        P("section", "dp", None),
        P("section", "dp", None),
        P("section", "dp", None),
        P("section", "dp", None),
        P("section", "dp", None),
    )
    return jax.shard_map(
        shards,
        mesh=mesh,
        in_specs=placed,
        out_specs=(
            P("section", "dp", None),
            P("section", "dp", None),
            P("section", "dp", None),
            P("section", "dp", None),
            P("section", "dp", None),
            P("section", "dp", None),
            P("section", "dp", None),
            P("section", None),
            P("section", "dp", None),
        ),
        check_vma=False,
    )
```

```python
import functools
import jax
import jax.numpy as jnp
from jax import lax
from jax.experimental import pallas as pl
from jax.experimental.pallas import tpu as pltpu
from jax.sharding import PartitionSpec as P

beta_one = 0.9
beta_two = 0.95
learn_rate = 0.002
decay_rate = 0.1
adam_steps = 100.0
norm_eps = 1e-06
adam_eps = 1e-08
scale_eps = 1e-06

RING = 4
CORES = 2
ROWS = 28
PAD = 32
PARTS = (64, 64, 64, 64)
F32 = jnp.float32
BF16 = jnp.bfloat16
NT = (((1,), (1,)), ((), ()))
NN = (((1,), (0,)), ((), ()))


def mm(a, b, dims=NN):
    return lax.dot_general(a, b, dims, preferred_element_type=F32)


def tiles(count, step=512):
    return [(i, min(step, count - i)) for i in range(0, count, step)]


def coords():
    dp = lax.axis_index("dp")
    chip = dp // CORES
    return chip // RING, chip % RING, dp % CORES


def dp_index(y, x, core):
    return (y * RING + x) * CORES + core


class Copies:
    def __init__(self, send_sem, recv_sem):
        self.send_sem, self.recv_sem = send_sem, recv_sem
        self.sent = []
        self.slots = {}

    def slot(self, key):
        return self.slots.setdefault(key, len(self.slots))

    def start(self, src, dst, key, device):
        copy = pltpu.make_async_remote_copy(
            src_ref=src,
            dst_ref=dst,
            send_sem=self.send_sem.at[len(self.sent)],
            recv_sem=self.recv_sem.at[self.slot(key)],
            device_id={"dp": device},
            device_id_type=pl.DeviceIdType.MESH,
        )
        copy.start()
        self.sent.append(copy)

    def wait_recv(self, dst, key):
        pltpu.make_async_remote_copy(
            src_ref=dst,
            dst_ref=dst,
            send_sem=self.send_sem.at[0],
            recv_sem=self.recv_sem.at[self.slot(key)],
            device_id={"dp": lax.axis_index("dp")},
            device_id_type=pl.DeviceIdType.MESH,
        ).wait_recv()

    def wait_sends(self):
        for copy in self.sent:
            copy.wait_send()


def plane_barrier(extra=()):
    y, x, core = coords()
    sem = pltpu.get_barrier_semaphore()
    for device in (
        dp_index((y + 1) % RING, x, core),
        dp_index((y + RING - 1) % RING, x, core),
        dp_index(y, (x + 1) % RING, core),
        dp_index(y, (x + RING - 1) % RING, core),
        dp_index(y, x, 1 - core),
    ):
        pl.semaphore_signal(sem, inc=1, device_id={"dp": device}, device_id_type=pl.DeviceIdType.MESH)
    for section in extra:
        pl.semaphore_signal(sem, inc=1, device_id={"section": section}, device_id_type=pl.DeviceIdType.MESH)
    pl.semaphore_wait(sem, 5 + len(extra))


def gather_steps(buf, copies, hidden):
    y, x, core = coords()

    def place(half, first, second):
        if half == 0:
            return (y + second) % RING, (x + first) % RING
        return (y + first) % RING, (x + second) % RING

    def piece(half, first, second, which, owner_core=None):
        py, px = place(half, first, second)
        base = dp_index(py, px, core if owner_core is None else owner_core) * PAD
        start, size = {None: (0, PAD), 0: (0, PAD // 2), 1: (PAD // 2, PAD // 2)}[which]
        start = pl.multiple_of(base + start, PAD // 2)
        return buf.at[pl.ds(start, size), pl.ds(half * hidden, hidden)]

    def send(half, first, second, which, axis, step):
        if axis == 0:
            py, px = place(half, step, 0)
            key = ("ag", half, (first - step) % RING, second, which)
        else:
            py, px = place(half, 0, step)
            key = ("ag", half, first, (second - step) % RING, which)
        ref = piece(half, first, second, which)
        copies.start(ref, ref, key, dp_index(py, px, core))

    def sibling(half, first, second):
        ref = piece(half, first, second, None)
        copies.start(ref, ref, ("sib", half, first, second), dp_index(y, x, 1 - core))

    def arrive(half, first, second):
        for which in (0, 1) if 2 in (first if second == 0 else second,) else (None,):
            copies.wait_recv(piece(half, first, second, which), ("ag", half, first, second, which))

    def spread(half, first):
        send(half, first, 0, None, 1, 1)
        send(half, first, 0, None, 1, -1)

    def on_first(half, first):
        arrive(half, first, 0)
        if first == 3:
            send(half, first, 0, 0, 0, 1)
        if first == 1:
            send(half, first, 0, 1, 0, -1)
        spread(half, first)
        sibling(half, first, 0)

    def on_second(half, first, second):
        arrive(half, first, second)
        if second == 3:
            send(half, first, second, 0, 1, 1)
        if second == 1:
            send(half, first, second, 1, 1, -1)
        sibling(half, first, second)

    def begin(half):
        send(half, 0, 0, None, 0, 1)
        send(half, 0, 0, None, 0, -1)
        spread(half, 0)
        sibling(half, 0, 0)

    def both(step, *key):
        return [functools.partial(step, half, *key) for half in (0, 1)]

    rounds = (
        both(on_first, 3) + both(on_first, 1),
        both(on_second, 0, 3) + both(on_second, 0, 1) + both(on_first, 2),
        both(on_second, 0, 2),
        both(on_second, 3, 3) + both(on_second, 3, 1) + both(on_second, 1, 3) + both(on_second, 1, 1),
        both(on_second, 3, 2) + both(on_second, 1, 2),
        both(on_second, 2, 3) + both(on_second, 2, 1),
        both(on_second, 2, 2),
    )

    def from_sibling(half, first, second):
        copies.wait_recv(piece(half, first, second, None, 1 - core), ("sib", half, first, second))

    return begin, rounds, from_sibling


def pad_matrix(ref, padded_axis):
    chunk = 128
    for start in range(0, ref.shape[0], chunk):
        shape = (chunk, ref.shape[1])
        ids = [lax.broadcasted_iota(jnp.int32, shape, axis) for axis in (0, 1)]
        ids[0] = ids[0] + start
        plain, number = ids[1 - padded_axis], ids[padded_axis]
        block, inner = number // PAD, number % PAD
        hit = jnp.logical_and(inner < ROWS, block * ROWS + inner == plain)
        ref[pl.ds(start, chunk), :] = jnp.where(hit, 1.0, 0.0).astype(BF16)


def rms(inputs):
    widened = inputs.astype(F32)
    return widened, lax.rsqrt(jnp.mean(widened * widened, axis=-1, keepdims=True) + norm_eps)


def back_kernel(
    own_ref, x_ref, cot_ref, gain_ref, scale_ref, down_ref,
    outgoing, rail_ref,
    weights, turned, down_raw, down_turned, spread, gather, normed_pad, wide_pad, inv_ref, gain_pad,
    slope_gate, slope_up, slope_sum, partial, upstream, grads, sides,
    send_sem, recv_sem, wave_send, wave_recv, local_sem,
):
    y, x, core = coords()
    section = lax.axis_index("section")
    sections = lax.axis_size("section")
    last = sections - 1
    tokens, features = x_ref.shape
    hidden = down_ref.shape[0]
    padded = gather.shape[0]
    rail = padded // CORES
    width = padded // RING
    copies = Copies(send_sem, recv_sem)
    fetch = pltpu.make_async_copy(down_ref, down_raw, local_sem)
    fetch.start()
    mine = pl.multiple_of(lax.axis_index("dp") * PAD, PAD)
    weights[pl.ds(mine, PAD), :] = own_ref[...]
    plane_barrier(((section + 1) % sections, (section + sections - 1) % sections))
    begin, rounds, from_sibling = gather_steps(weights, copies, hidden)
    begin(0)
    begin(1)

    pad_matrix(spread, 1)
    one_hot = spread[...]
    widened, inverse = rms(x_ref[...])
    gain = gain_ref[...]
    normed = (widened * inverse * gain).astype(BF16)
    inv_ref[...] = inverse
    high = gain.astype(BF16)
    rest = gain - high.astype(F32)
    middle = rest.astype(BF16)
    low = (rest - middle.astype(F32)).astype(BF16)
    gain_pad[...] = mm(high, one_hot) + mm(middle, one_hot) + mm(low, one_hot)
    wide_pad[...] = mm(x_ref[...], one_hot)
    normed_pad[...] = mm(normed, one_hot).astype(BF16)

    flat = normed_pad[...].T.reshape(padded // (CORES * PAD), CORES, PAD, tokens)
    even = flat[:, 0].reshape(rail, tokens)
    odd = flat[:, 1].reshape(rail, tokens)
    sides[:, pl.ds(0, tokens)] = jnp.where(core == 0, even, odd)
    sides[:, pl.ds(2 * tokens, tokens)] = jnp.where(core == 0, odd, even)
    other = dp_index(y, x, 1 - core)
    copies.start(
        sides.at[:, pl.ds(2 * tokens, tokens)], sides.at[:, pl.ds(tokens, tokens)], "side", other
    )

    def down_piece(start, size):
        down_turned[:, pl.ds(start, size)] = mm(
            gather[...], down_raw[pl.ds(start, size), :], NT
        ).astype(BF16)

    def weight_rows(half, step):
        for i in range(RING):
            from_sibling(half, *((i, step) if half == 0 else (step, i)))
        rows = pl.ds(pl.multiple_of(((y + step) % RING) * width, width), width)
        target = (slope_gate, slope_up)[half]
        left = normed_pad[:, rows]
        for start, size in tiles(hidden):
            here = weights[rows, pl.ds(half * hidden + start, size)]
            turned[pl.ds(half * hidden + start, size), rows] = here.T
            product = mm(left, here)
            cols = pl.ds(start, size)
            target[:, cols] = product if step == 0 else target[:, cols] + product

    downs = [functools.partial(down_piece, *piece) for piece in tiles(hidden, 256)]

    def run(items):
        for item in items:
            item()
            if downs:
                downs.pop(0)()

    run_plain = lambda items: [item() for item in items]
    run_plain(rounds[0])
    pad_matrix(gather, 0)
    fetch.wait()

    @pl.when(section == last)
    def _():
        upstream[...] = mm(cot_ref[...], one_hot).astype(BF16)

    run(rounds[1])
    run(rounds[2])
    weight_rows(0, 0)
    weight_rows(1, 0)
    run(rounds[3])
    while downs:
        downs.pop(0)()
    run(rounds[4])
    weight_rows(1, 3)
    run(rounds[5])
    weight_rows(1, 1)
    run(rounds[6])
    weight_rows(0, 3)
    weight_rows(0, 1)
    weight_rows(0, 2)
    weight_rows(1, 2)

    parts = []
    for size in PARTS:
        parts.append((sum(PARTS[: len(parts)]), size))

    def slopes(first, count):
        rows = pl.ds(first, count)
        for start, size in tiles(hidden):
            cols = pl.ds(start, size)
            gate = slope_gate[rows, cols] * scale_ref[0, 0]
            up = slope_up[rows, cols] * scale_ref[0, 1]
            sigmoid = 1.0 / (1.0 + jnp.exp(-gate))
            by_gate = up * (sigmoid * (1.0 + gate * (1.0 - sigmoid)))
            by_up = gate * sigmoid
            slope_gate[rows, cols] = by_gate
            slope_up[rows, cols] = by_up
            slope_sum[rows, cols] = by_gate * gate + by_up * up

    slopes(*parts[0])

    @pl.when(section < last)
    def _():
        slopes(parts[1][0], tokens - parts[1][0])

    def wave_copy(part, piece):
        rows, cols = pl.ds(*parts[part]), pl.ds(piece * width, width)
        return pltpu.make_async_remote_copy(
            src_ref=outgoing.at[rows, cols],
            dst_ref=upstream.at[rows, cols],
            send_sem=wave_send.at[part * RING + piece],
            recv_sem=wave_recv.at[part * RING + piece],
            device_id={"section": jnp.maximum(section - 1, 0)},
            device_id_type=pl.DeviceIdType.MESH,
        )

    for part, (first, count) in enumerate(parts):
        rows = pl.ds(first, count)
        if part > 0:

            @pl.when(section == last)
            def _():
                slopes(first, count)

        sums = jnp.zeros((count, 128), F32)
        for piece in range(RING):
            span = pl.ds(piece * width, width)

            @pl.when(section < last)
            def _():
                wave_copy(part, piece).wait_recv()

            left = upstream[rows, span]
            for start, size in tiles(hidden):
                cols = pl.ds(start, size)
                product = mm(left, down_turned[span, cols])
                if piece > 0:
                    product = product + partial[pl.ds(0, count), cols]
                if piece < RING - 1:
                    partial[pl.ds(0, count), cols] = product
                    continue
                grads[rows, cols] = (product * slope_gate[rows, cols]).astype(BF16)
                grads[rows, pl.ds(hidden + start, size)] = (product * slope_up[rows, cols]).astype(BF16)
                product = product * slope_sum[rows, cols]
                for lane in range(0, size, 128):
                    sums = sums + product[:, lane : lane + 128]
        copies.start(grads.at[rows], grads.at[pl.ds(tokens + first, count)], ("grads", part), other)
        inverse = inv_ref[rows, :]
        mean = jnp.sum(sums, axis=-1, keepdims=True) * (inverse * inverse / features)
        for piece in range(RING):
            span = pl.ds(piece * width, width)
            normed_grad = (
                mm(grads[rows, pl.ds(0, hidden)], turned[pl.ds(0, hidden), span]) * scale_ref[0, 0]
                + mm(grads[rows, pl.ds(hidden, hidden)], turned[pl.ds(hidden, hidden), span])
                * scale_ref[0, 1]
            )
            outgoing[rows, span] = (
                upstream[rows, span].astype(F32)
                + inverse * (gain_pad[:, span] * normed_grad)
                - wide_pad[rows, span] * mean
            ).astype(BF16)

            @pl.when(section > 0)
            def _():
                wave_copy(part, piece).start()

    copies.wait_recv(sides.at[:, pl.ds(tokens, tokens)], "side")
    for part, (first, count) in enumerate(parts):
        copies.wait_recv(grads.at[pl.ds(tokens + first, count)], ("grads", part))
    both = sides[:, pl.ds(0, 2 * tokens)]
    for start, size in tiles(2 * hidden):
        cols = pl.ds(start, size)
        rail_ref[:, cols] = mm(both, grads[:, cols]).astype(BF16)

    @pl.when(section > 0)
    def _():
        for part in range(len(parts)):
            for piece in range(RING):
                wave_copy(part, piece).wait_send()

    copies.wait_sends()


def adam_update(master, moment_old, second_old, gradient):
    moment_one = beta_one * moment_old + (1.0 - beta_one) * gradient
    moment_two = beta_two * second_old + (1.0 - beta_two) * gradient * gradient
    unbiased_one = moment_one / (1.0 - beta_one**adam_steps)
    unbiased_two = moment_two / (1.0 - beta_two**adam_steps)
    updated = master - learn_rate * (
        unbiased_one / (jnp.sqrt(unbiased_two) + adam_eps) + decay_rate * master
    )
    return (updated, moment_one, moment_two)


def reduce_steps(rail, near, whole, near_last, whole_last, copies, hidden):
    y, x, core = coords()

    def place(half, bulk, other):
        if half == 0:
            return (y + bulk) % RING, (x + other) % RING
        return (y + other) % RING, (x + bulk) % RING

    def block(half, bulk, other, which=None):
        py, px = place(half, bulk, other)
        start, size = {None: (0, PAD), 0: (0, PAD // 2), 1: (PAD // 2, PAD // 2)}[which]
        start = pl.multiple_of((py * RING + px) * PAD + start, PAD // 2)
        return rail.at[pl.ds(start, size), pl.ds(half * hidden, hidden)]

    def send(src, dst, key, half, axis, step):
        py, px = place(half, step, 0) if axis == 0 else place(half, 0, step)
        copies.start(src, dst, key, dp_index(py, px, core))

    def far(half, other):
        for which, step in ((0, 1), (1, -1)):
            send(block(half, 2, other, which), near.at[half, other, which], ("n", half, other, which), half, 0, step)

    def pass_on(half, other):
        for which, step in ((0, 1), (1, -1)):
            copies.wait_recv(near.at[half, other, which], ("n", half, other, which))
            ref = block(half, step, other, which)
            ref[...] = (ref[...].astype(F32) + near[half, other, which].astype(F32)).astype(BF16)
            send(block(half, step, other), whole.at[half, other, which], ("w", half, other, which), half, 0, step)

    def settle(half, other):
        for which in (0, 1):
            copies.wait_recv(whole.at[half, other, which], ("w", half, other, which))
        ref = block(half, 0, other)
        ref[...] = (
            ref[...].astype(F32) + whole[half, other, 0].astype(F32) + whole[half, other, 1].astype(F32)
        ).astype(BF16)

    def far_last(half):
        for which, step in ((0, 1), (1, -1)):
            send(block(half, 0, 2, which), near_last.at[half, which], ("nl", half, which), half, 1, step)

    def pass_last(half):
        for which, step in ((0, 1), (1, -1)):
            copies.wait_recv(near_last.at[half, which], ("nl", half, which))
            ref = block(half, 0, step, which)
            ref[...] = (ref[...].astype(F32) + near_last[half, which].astype(F32)).astype(BF16)
            send(block(half, 0, step), whole_last.at[half, which], ("wl", half, which), half, 1, step)

    def total(half):
        for which in (0, 1):
            copies.wait_recv(whole_last.at[half, which], ("wl", half, which))
        return (
            block(half, 0, 0)[...].astype(F32)
            + whole_last[half, 0].astype(F32)
            + whole_last[half, 1].astype(F32)
        )

    return far, pass_on, settle, far_last, pass_last, total


def update_kernel(
    rail_ref, back_ref, next_ref, gain_ref, mg_ref, mu_ref, og_ref, ou_ref, sg_ref, su_ref,
    result_ref, out_ref, nmg_ref, nmu_ref, nog_ref, nou_ref, nsg_ref, nsu_ref, scale_ref,
    weights, rail, near, whole, near_last, whole_last, spread, gather, next_pad, block_ref, flat_ref,
    state, updates, send_sem, recv_sem, local_sem, state_sem,
):
    y, x, core = coords()
    hidden = out_ref.shape[1]
    features = next_ref.shape[1]
    copies = Copies(send_sem, recv_sem)
    fetch = pltpu.make_async_copy(rail_ref, rail, local_sem)
    fetch.start()
    loads = [
        pltpu.make_async_copy(ref.at[:, 0, :], state.at[i], state_sem.at[i])
        for i, ref in enumerate((mg_ref, mu_ref, og_ref, ou_ref, sg_ref, su_ref))
    ]
    for load in loads:
        load.start()
    plane_barrier()
    fetch.wait()
    far, pass_on, settle, far_last, pass_last, total = reduce_steps(
        rail, near, whole, near_last, whole_last, copies, hidden
    )
    order = (2, 1, 3, 0)
    for other in order:
        far(0, other)
        far(1, other)
    pad_matrix(spread, 1)
    widened, inverse = rms(next_ref[...])
    next_normed = (widened * inverse * gain_ref[...]).astype(BF16)
    next_pad[...] = mm(next_normed, spread[...]).astype(BF16)
    pad_matrix(gather, 0)
    result_ref[...] = mm(back_ref[...], gather[...]).astype(BF16)
    for other in order:
        pass_on(0, other)
        pass_on(1, other)
    for other in order:
        settle(0, other)
        settle(1, other)
        if other == 2:
            far_last(0)
            far_last(1)
    pass_last(0)
    pass_last(1)

    begin, rounds, from_sibling = gather_steps(weights, copies, hidden)
    lanes = flat_ref.shape[1]
    lines = hidden // lanes
    mine = pl.multiple_of(lax.axis_index("dp") * PAD, PAD)
    for load in loads:
        load.wait()
    stores = []
    for half, outs in ((0, (nmg_ref, nog_ref, nsg_ref)), (1, (nmu_ref, nou_ref, nsu_ref))):
        gradient = total(half)
        for line in range(lines):
            flat_ref[pl.ds(line, ROWS, stride=lines), :] = gradient[:ROWS, line * lanes : (line + 1) * lanes]
        gradient = flat_ref[...]
        results = adam_update(state[half], state[2 + half], state[4 + half], gradient)
        for i, value in enumerate(results):
            number = 2 * i + half
            updates[number] = value
            stores.append(
                pltpu.make_async_copy(updates.at[number], outs[i].at[:, 0, :], state_sem.at[number])
            )
            stores[-1].start()
        updated = results[0]
        peak = jnp.max(jnp.abs(updated), keepdims=True)
        high = peak.astype(BF16).astype(F32)
        middle = (peak - high).astype(BF16).astype(F32)
        low = peak - high - middle
        tail = lax.broadcasted_iota(jnp.int32, (PAD - ROWS, hidden), 0)
        for line in range(lines):
            block_ref[pl.ds(0, ROWS), pl.ds(line * lanes, lanes)] = updates[half, pl.ds(line, ROWS, stride=lines), :]
        block_ref[pl.ds(ROWS, PAD - ROWS), :] = jnp.where(
            tail == 0, high, jnp.where(tail == 1, middle, jnp.where(tail == 2, low, 0.0))
        )
        weights[pl.ds(mine, PAD), pl.ds(half * hidden, hidden)] = block_ref[...].astype(BF16)
        begin(half)
    for group in rounds:
        for step in group:
            step()
    for first in range(RING):
        for second in range(RING):
            from_sibling(0, first, second)
            from_sibling(1, first, second)

    peaks = []
    for half in (0, 1):
        heads = weights[:, pl.ds(half * hidden, 128)].astype(F32)
        heads = heads.reshape(heads.shape[0] // PAD, PAD, 128)[:, PAD - 8 :, :]
        level = lax.broadcasted_iota(jnp.int32, heads.shape, 1)
        found = jnp.sum(jnp.where(level >= 4, heads, 0.0), axis=1)
        peaks.append(jnp.max(found, keepdims=True) + scale_eps)
    lane = lax.broadcasted_iota(jnp.int32, scale_ref.shape, 1)
    scale_ref[...] = jnp.where(lane == 0, peaks[0], peaks[1])
    for start, size in tiles(hidden):
        cols = pl.ds(start, size)
        gate = mm(next_pad[...], weights[:, cols])
        up = mm(next_pad[...], weights[:, pl.ds(hidden + start, size)])
        out_ref[:, cols] = (gate / (1.0 + jnp.exp(-gate)) * up).astype(BF16)
    for store in stores:
        store.wait()
    copies.wait_sends()


VMEM = pl.BlockSpec(memory_space=pltpu.VMEM)
SMEM = pl.BlockSpec(memory_space=pltpu.SMEM)
ANY = pl.BlockSpec(memory_space=pl.ANY)


def shards(
    section_inputs,
    cotangent,
    norm_gain,
    quant_gate,
    quant_up,
    scales,
    down_proj,
    master_gate,
    master_up,
    moment_gate,
    moment_up,
    second_gate,
    second_up,
    next_inputs,
):
    tokens, features = cotangent.shape
    hidden = quant_gate.shape[2]
    partners = lax.axis_size("dp")
    padded = partners * PAD
    rail_rows = padded // CORES
    own = jnp.pad(
        jnp.concatenate([quant_gate[0], quant_up[0]], axis=1), ((0, PAD - ROWS), (0, 0))
    )
    dma = pltpu.SemaphoreType.DMA
    back, rail = pl.pallas_call(
        back_kernel,
        out_shape=(
            jax.ShapeDtypeStruct((tokens, padded), BF16),
            jax.ShapeDtypeStruct((rail_rows, 2 * hidden), BF16),
        ),
        in_specs=[VMEM, VMEM, VMEM, VMEM, SMEM, ANY],
        out_specs=(VMEM, VMEM),
        scratch_shapes=[
            pltpu.VMEM((padded, 2 * hidden), BF16),
            pltpu.VMEM((2 * hidden, padded), BF16),
            pltpu.VMEM((hidden, features), BF16),
            pltpu.VMEM((padded, hidden), BF16),
            pltpu.VMEM((features, padded), BF16),
            pltpu.VMEM((padded, features), BF16),
            pltpu.VMEM((tokens, padded), BF16),
            pltpu.VMEM((tokens, padded), F32),
            pltpu.VMEM((tokens, 1), F32),
            pltpu.VMEM((1, padded), F32),
            pltpu.VMEM((tokens, hidden), F32),
            pltpu.VMEM((tokens, hidden), F32),
            pltpu.VMEM((tokens, hidden), F32),
            pltpu.VMEM((max(PARTS), hidden), F32),
            pltpu.VMEM((tokens, padded), BF16),
            pltpu.VMEM((2 * tokens, 2 * hidden), BF16),
            pltpu.VMEM((rail_rows, 3 * tokens), BF16),
            dma((80,)),
            dma((80,)),
            dma((len(PARTS) * RING,)),
            dma((len(PARTS) * RING,)),
            dma(()),
        ],
        compiler_params=pltpu.CompilerParams(
            collective_id=0, has_side_effects=True, vmem_limit_bytes=60 * 2**20
        ),
    )(own, section_inputs[0], cotangent, norm_gain, scales, down_proj[0])
    lanes = 128
    lines = ROWS * hidden // lanes
    row = jax.ShapeDtypeStruct((lines, 1, lanes), F32)
    flat = [
        value.transpose(1, 0, 2).reshape(row.shape)
        for value in (master_gate, master_up, moment_gate, moment_up, second_gate, second_up)
    ]
    outs = pl.pallas_call(
        update_kernel,
        out_shape=(
            jax.ShapeDtypeStruct((tokens, features), BF16),
            jax.ShapeDtypeStruct((tokens, hidden), BF16),
        )
        + (row,) * 6
        + (jax.ShapeDtypeStruct((1, 2), F32),),
        in_specs=[ANY] + [VMEM] * 3 + [ANY] * 6,
        out_specs=(VMEM,) * 2 + (ANY,) * 6 + (VMEM,),
        scratch_shapes=[
            pltpu.VMEM((padded, 2 * hidden), BF16),
            pltpu.VMEM((rail_rows, 2 * hidden), BF16),
            pltpu.VMEM((2, RING, 2, PAD // 2, hidden), BF16),
            pltpu.VMEM((2, RING, 2, PAD, hidden), BF16),
            pltpu.VMEM((2, 2, PAD // 2, hidden), BF16),
            pltpu.VMEM((2, 2, PAD, hidden), BF16),
            pltpu.VMEM((features, padded), BF16),
            pltpu.VMEM((padded, features), BF16),
            pltpu.VMEM((tokens, padded), BF16),
            pltpu.VMEM((PAD, hidden), F32),
            pltpu.VMEM((lines, lanes), F32),
            pltpu.VMEM((6, lines, lanes), F32),
            pltpu.VMEM((6, lines, lanes), F32),
            dma((128,)),
            dma((128,)),
            dma(()),
            dma((6,)),
        ],
        compiler_params=pltpu.CompilerParams(
            collective_id=1, has_side_effects=True, vmem_limit_bytes=60 * 2**20
        ),
    )(rail, back, next_inputs[0], norm_gain, *flat)
    result, next_hidden = outs[:2]
    return (
        (result[None],)
        + tuple(value.reshape(ROWS, 1, hidden).transpose(1, 0, 2) for value in outs[2:8])
        + (outs[8], next_hidden[None])
    )


def solution(mesh):
    placed = (
        P("section", "dp", None),
        P("dp", None),
        P("section", None),
        P("section", "dp", None),
        P("section", "dp", None),
        P("section", None),
        P("section", None, None),
        P("section", "dp", None),
        P("section", "dp", None),
        P("section", "dp", None),
        P("section", "dp", None),
        P("section", "dp", None),
        P("section", "dp", None),
        P("section", "dp", None),
    )
    return jax.shard_map(
        shards,
        mesh=mesh,
        in_specs=placed,
        out_specs=(
            P("section", "dp", None),
            P("section", "dp", None),
            P("section", "dp", None),
            P("section", "dp", None),
            P("section", "dp", None),
            P("section", "dp", None),
            P("section", "dp", None),
            P("section", None),
            P("section", "dp", None),
        ),
        check_vma=False,
    )
```

```python
import functools
import jax
import jax.numpy as jnp
from jax import lax
from jax.experimental import pallas as pl
from jax.experimental.pallas import tpu as pltpu
from jax.sharding import PartitionSpec as P

beta_one = 0.9
beta_two = 0.95
learn_rate = 0.002
decay_rate = 0.1
adam_steps = 100.0
norm_eps = 1e-06
adam_eps = 1e-08
scale_eps = 1e-06

RING = 4
CORES = 2
ROWS = 28
PAD = 32
PARTS = (64, 64, 64, 64)
F32 = jnp.float32
BF16 = jnp.bfloat16
NT = (((1,), (1,)), ((), ()))
NN = (((1,), (0,)), ((), ()))


def mm(a, b, dims=NN):
    return lax.dot_general(a, b, dims, preferred_element_type=F32)


def tiles(count, step=512):
    return [(i, min(step, count - i)) for i in range(0, count, step)]


def coords():
    dp = lax.axis_index("dp")
    chip = dp // CORES
    return chip // RING, chip % RING, dp % CORES


def dp_index(y, x, core):
    return (y * RING + x) * CORES + core


class Copies:
    def __init__(self, send_sem, recv_sem):
        self.send_sem, self.recv_sem = send_sem, recv_sem
        self.sent = []
        self.slots = {}

    def slot(self, key):
        return self.slots.setdefault(key, len(self.slots))

    def start(self, src, dst, key, device):
        copy = pltpu.make_async_remote_copy(
            src_ref=src,
            dst_ref=dst,
            send_sem=self.send_sem.at[len(self.sent)],
            recv_sem=self.recv_sem.at[self.slot(key)],
            device_id={"dp": device},
            device_id_type=pl.DeviceIdType.MESH,
        )
        copy.start()
        self.sent.append(copy)

    def wait_recv(self, dst, key):
        pltpu.make_async_remote_copy(
            src_ref=dst,
            dst_ref=dst,
            send_sem=self.send_sem.at[0],
            recv_sem=self.recv_sem.at[self.slot(key)],
            device_id={"dp": lax.axis_index("dp")},
            device_id_type=pl.DeviceIdType.MESH,
        ).wait_recv()

    def wait_sends(self):
        for copy in self.sent:
            copy.wait_send()


def plane_barrier(extra=()):
    y, x, core = coords()
    sem = pltpu.get_barrier_semaphore()
    for device in (
        dp_index((y + 1) % RING, x, core),
        dp_index((y + RING - 1) % RING, x, core),
        dp_index(y, (x + 1) % RING, core),
        dp_index(y, (x + RING - 1) % RING, core),
        dp_index(y, x, 1 - core),
    ):
        pl.semaphore_signal(sem, inc=1, device_id={"dp": device}, device_id_type=pl.DeviceIdType.MESH)
    for section in extra:
        pl.semaphore_signal(sem, inc=1, device_id={"section": section}, device_id_type=pl.DeviceIdType.MESH)
    pl.semaphore_wait(sem, 5 + len(extra))


def gather_steps(buf, copies, hidden):
    y, x, core = coords()

    def place(half, first, second):
        if half == 0:
            return (y + second) % RING, (x + first) % RING
        return (y + first) % RING, (x + second) % RING

    def piece(half, first, second, which, owner_core=None):
        py, px = place(half, first, second)
        base = dp_index(py, px, core if owner_core is None else owner_core) * PAD
        start, size = {None: (0, PAD), 0: (0, PAD // 2), 1: (PAD // 2, PAD // 2)}[which]
        start = pl.multiple_of(base + start, PAD // 2)
        return buf.at[pl.ds(start, size), pl.ds(half * hidden, hidden)]

    def send(half, first, second, which, axis, step):
        if axis == 0:
            py, px = place(half, step, 0)
            key = ("ag", half, (first - step) % RING, second, which)
        else:
            py, px = place(half, 0, step)
            key = ("ag", half, first, (second - step) % RING, which)
        ref = piece(half, first, second, which)
        copies.start(ref, ref, key, dp_index(py, px, core))

    def sibling(half, first, second):
        ref = piece(half, first, second, None)
        copies.start(ref, ref, ("sib", half, first, second), dp_index(y, x, 1 - core))

    def arrive(half, first, second):
        for which in (0, 1) if 2 in (first if second == 0 else second,) else (None,):
            copies.wait_recv(piece(half, first, second, which), ("ag", half, first, second, which))

    def bulk(half, first):
        send(half, first, 0, None, 1, 1)
        send(half, first, 0, None, 1, -1)

    def relay(half, first, second):
        arrive(half, first, second)
        axis = 0 if second == 0 else 1
        if (first, second)[axis] == 3:
            send(half, first, second, 0, axis, 1)
        else:
            send(half, first, second, 1, axis, -1)

    def begin(half):
        send(half, 0, 0, None, 0, 1)
        send(half, 0, 0, None, 0, -1)
        bulk(half, 0)
        sibling(half, 0, 0)

    def group(*steps):
        return [functools.partial(step, half, *key) for step, *key in steps for half in (0, 1)]

    def lines(first, *more):
        return group(
            (relay, first, 3), (relay, first, 1), *more, (sibling, first, 3), (sibling, first, 1)
        )

    def opposite(first, second):
        return group((arrive, first, second), (sibling, first, second))

    rounds = (
        group((relay, 3, 0), (relay, 1, 0), (bulk, 3), (sibling, 3, 0), (sibling, 1, 0)),
        lines(0, (bulk, 1)),
        opposite(2, 0),
        lines(3, (bulk, 2)),
        opposite(0, 2),
        lines(1),
        opposite(3, 2),
        lines(2),
        opposite(1, 2),
        opposite(2, 2),
    )

    def from_sibling(half, first, second):
        copies.wait_recv(piece(half, first, second, None, 1 - core), ("sib", half, first, second))

    return begin, rounds, from_sibling


def pad_matrix(ref, padded_axis):
    chunk = 128
    for start in range(0, ref.shape[0], chunk):
        shape = (chunk, ref.shape[1])
        ids = [lax.broadcasted_iota(jnp.int32, shape, axis) for axis in (0, 1)]
        ids[0] = ids[0] + start
        plain, number = ids[1 - padded_axis], ids[padded_axis]
        block, inner = number // PAD, number % PAD
        hit = jnp.logical_and(inner < ROWS, block * ROWS + inner == plain)
        ref[pl.ds(start, chunk), :] = jnp.where(hit, 1.0, 0.0).astype(BF16)


def rms(inputs):
    widened = inputs.astype(F32)
    return widened, lax.rsqrt(jnp.mean(widened * widened, axis=-1, keepdims=True) + norm_eps)


def back_kernel(
    gate_ref, up_ref, x_ref, cot_ref, gain_ref, scale_ref, down_ref,
    outgoing, rail_ref,
    weights, turned, down_raw, down_turned, spread, gather, normed_pad, wide_pad, inv_ref, gain_pad,
    slope_gate, slope_up, slope_sum, partial, upstream, grads, sides, block,
    send_sem, recv_sem, wave_send, wave_recv, local_sem,
):
    y, x, core = coords()
    section = lax.axis_index("section")
    sections = lax.axis_size("section")
    last = sections - 1
    tokens, features = x_ref.shape
    hidden = down_ref.shape[0]
    padded = gather.shape[0]
    rail = padded // CORES
    width = padded // RING
    copies = Copies(send_sem, recv_sem)
    fetch = pltpu.make_async_copy(down_ref, down_raw, local_sem)
    fetch.start()
    mine = pl.multiple_of(lax.axis_index("dp") * PAD, PAD)
    block[...] = jnp.zeros(block.shape, BF16)
    block[pl.ds(0, ROWS), pl.ds(0, hidden)] = gate_ref[...]
    block[pl.ds(0, ROWS), pl.ds(hidden, hidden)] = up_ref[...]
    weights[pl.ds(mine, PAD), :] = block[...]
    plane_barrier(((section + 1) % sections, (section + sections - 1) % sections))
    begin, rounds, from_sibling = gather_steps(weights, copies, hidden)
    begin(0)
    begin(1)

    pad_matrix(spread, 1)
    one_hot = spread[...]
    widened, inverse = rms(x_ref[...])
    gain = gain_ref[...]
    normed = (widened * inverse * gain).astype(BF16)
    inv_ref[...] = inverse
    high = gain.astype(BF16)
    rest = gain - high.astype(F32)
    middle = rest.astype(BF16)
    low = (rest - middle.astype(F32)).astype(BF16)
    gain_pad[...] = mm(high, one_hot) + mm(middle, one_hot) + mm(low, one_hot)
    wide_pad[...] = mm(x_ref[...], one_hot)
    normed_pad[...] = mm(normed, one_hot).astype(BF16)

    flat = normed_pad[...].T.reshape(padded // (CORES * PAD), CORES, PAD, tokens)
    even = flat[:, 0].reshape(rail, tokens)
    odd = flat[:, 1].reshape(rail, tokens)
    sides[:, pl.ds(0, tokens)] = jnp.where(core == 0, even, odd)
    sides[:, pl.ds(2 * tokens, tokens)] = jnp.where(core == 0, odd, even)
    other = dp_index(y, x, 1 - core)
    copies.start(
        sides.at[:, pl.ds(2 * tokens, tokens)], sides.at[:, pl.ds(tokens, tokens)], "side", other
    )

    def down_piece(start, size):
        down_turned[:, pl.ds(start, size)] = mm(
            gather[...], down_raw[pl.ds(start, size), :], NT
        ).astype(BF16)

    def weight_rows(half, step):
        for i in range(RING):
            from_sibling(half, *((i, step) if half == 0 else (step, i)))
        rows = pl.ds(pl.multiple_of(((y + step) % RING) * width, width), width)
        target = (slope_gate, slope_up)[half]
        left = normed_pad[:, rows]
        for start, size in tiles(hidden):
            here = weights[rows, pl.ds(half * hidden + start, size)]
            turned[pl.ds(half * hidden + start, size), rows] = here.T
            product = mm(left, here)
            cols = pl.ds(start, size)
            target[:, cols] = product if step == 0 else target[:, cols] + product

    downs = [functools.partial(down_piece, *piece) for piece in tiles(hidden, 256)]

    def run(items, count=0):
        for item in items:
            item()
        for _ in range(count):
            downs.pop(0)()

    run(rounds[0])
    pad_matrix(gather, 0)
    fetch.wait()

    @pl.when(section == last)
    def _():
        upstream[...] = mm(cot_ref[...], one_hot).astype(BF16)

    run(rounds[1], 2)
    run(rounds[2])
    weight_rows(0, 0)
    run(rounds[3], 3)
    run(rounds[4])
    weight_rows(1, 0)
    run(rounds[5], 3)
    run(rounds[6])
    weight_rows(1, 3)
    run(rounds[7], len(downs))
    run(rounds[8])
    weight_rows(1, 1)
    run(rounds[9])
    weight_rows(0, 3)
    weight_rows(0, 1)
    weight_rows(0, 2)
    weight_rows(1, 2)

    parts = []
    for size in PARTS:
        parts.append((sum(PARTS[: len(parts)]), size))

    def slopes(first, count):
        rows = pl.ds(first, count)
        for start, size in tiles(hidden):
            cols = pl.ds(start, size)
            gate = slope_gate[rows, cols] * scale_ref[0, 0]
            up = slope_up[rows, cols] * scale_ref[0, 1]
            sigmoid = 1.0 / (1.0 + jnp.exp(-gate))
            by_gate = up * (sigmoid * (1.0 + gate * (1.0 - sigmoid)))
            by_up = gate * sigmoid
            slope_gate[rows, cols] = by_gate
            slope_up[rows, cols] = by_up
            slope_sum[rows, cols] = by_gate * gate + by_up * up

    slopes(*parts[0])

    @pl.when(section < last)
    def _():
        slopes(parts[1][0], tokens - parts[1][0])

    def wave_copy(part, piece):
        rows, cols = pl.ds(*parts[part]), pl.ds(piece * width, width)
        return pltpu.make_async_remote_copy(
            src_ref=outgoing.at[rows, cols],
            dst_ref=upstream.at[rows, cols],
            send_sem=wave_send.at[part * RING + piece],
            recv_sem=wave_recv.at[part * RING + piece],
            device_id={"section": jnp.maximum(section - 1, 0)},
            device_id_type=pl.DeviceIdType.MESH,
        )

    for part, (first, count) in enumerate(parts):
        rows = pl.ds(first, count)
        if part > 0:

            @pl.when(section == last)
            def _():
                slopes(first, count)

        sums = jnp.zeros((count, 128), F32)
        for piece in range(RING):
            span = pl.ds(piece * width, width)

            @pl.when(section < last)
            def _():
                wave_copy(part, piece).wait_recv()

            left = upstream[rows, span]
            for start, size in tiles(hidden):
                cols = pl.ds(start, size)
                product = mm(left, down_turned[span, cols])
                if piece > 0:
                    product = product + partial[pl.ds(0, count), cols]
                if piece < RING - 1:
                    partial[pl.ds(0, count), cols] = product
                    continue
                grads[rows, cols] = (product * slope_gate[rows, cols]).astype(BF16)
                grads[rows, pl.ds(hidden + start, size)] = (product * slope_up[rows, cols]).astype(BF16)
                product = product * slope_sum[rows, cols]
                for lane in range(0, size, 128):
                    sums = sums + product[:, lane : lane + 128]
        copies.start(grads.at[rows], grads.at[pl.ds(tokens + first, count)], ("grads", part), other)
        inverse = inv_ref[rows, :]
        mean = jnp.sum(sums, axis=-1, keepdims=True) * (inverse * inverse / features)
        for piece in range(RING):
            span = pl.ds(piece * width, width)
            normed_grad = (
                mm(grads[rows, pl.ds(0, hidden)], turned[pl.ds(0, hidden), span]) * scale_ref[0, 0]
                + mm(grads[rows, pl.ds(hidden, hidden)], turned[pl.ds(hidden, hidden), span])
                * scale_ref[0, 1]
            )
            outgoing[rows, span] = (
                upstream[rows, span].astype(F32)
                + inverse * (gain_pad[:, span] * normed_grad)
                - wide_pad[rows, span] * mean
            ).astype(BF16)

            @pl.when(section > 0)
            def _():
                wave_copy(part, piece).start()

    copies.wait_recv(sides.at[:, pl.ds(tokens, tokens)], "side")
    for part, (first, count) in enumerate(parts):
        copies.wait_recv(grads.at[pl.ds(tokens + first, count)], ("grads", part))
    both = sides[:, pl.ds(0, 2 * tokens)]
    for start, size in tiles(2 * hidden):
        cols = pl.ds(start, size)
        rail_ref[:, cols] = mm(both, grads[:, cols]).astype(BF16)

    @pl.when(section > 0)
    def _():
        for part in range(len(parts)):
            for piece in range(RING):
                wave_copy(part, piece).wait_send()

    copies.wait_sends()


def adam_update(master, moment_old, second_old, gradient):
    moment_one = beta_one * moment_old + (1.0 - beta_one) * gradient
    moment_two = beta_two * second_old + (1.0 - beta_two) * gradient * gradient
    unbiased_one = moment_one / (1.0 - beta_one**adam_steps)
    unbiased_two = moment_two / (1.0 - beta_two**adam_steps)
    updated = master - learn_rate * (
        unbiased_one / (jnp.sqrt(unbiased_two) + adam_eps) + decay_rate * master
    )
    return (updated, moment_one, moment_two)


def reduce_steps(rail, near, whole, near_last, whole_last, copies, hidden):
    y, x, core = coords()

    def place(half, bulk, other):
        if half == 0:
            return (y + bulk) % RING, (x + other) % RING
        return (y + other) % RING, (x + bulk) % RING

    def block(half, bulk, other, which=None):
        py, px = place(half, bulk, other)
        start, size = {None: (0, PAD), 0: (0, PAD // 2), 1: (PAD // 2, PAD // 2)}[which]
        start = pl.multiple_of((py * RING + px) * PAD + start, PAD // 2)
        return rail.at[pl.ds(start, size), pl.ds(half * hidden, hidden)]

    def send(src, dst, key, half, axis, step):
        py, px = place(half, step, 0) if axis == 0 else place(half, 0, step)
        copies.start(src, dst, key, dp_index(py, px, core))

    def far(half, other):
        for which, step in ((0, 1), (1, -1)):
            send(block(half, 2, other, which), near.at[half, other, which], ("n", half, other, which), half, 0, step)

    def pass_on(half, other):
        for which, step in ((0, 1), (1, -1)):
            copies.wait_recv(near.at[half, other, which], ("n", half, other, which))
            ref = block(half, step, other, which)
            ref[...] = (ref[...].astype(F32) + near[half, other, which].astype(F32)).astype(BF16)
            send(block(half, step, other), whole.at[half, other, which], ("w", half, other, which), half, 0, step)

    def settle(half, other):
        for which in (0, 1):
            copies.wait_recv(whole.at[half, other, which], ("w", half, other, which))
        ref = block(half, 0, other)
        ref[...] = (
            ref[...].astype(F32) + whole[half, other, 0].astype(F32) + whole[half, other, 1].astype(F32)
        ).astype(BF16)

    def far_last(half):
        for which, step in ((0, 1), (1, -1)):
            send(block(half, 0, 2, which), near_last.at[half, which], ("nl", half, which), half, 1, step)

    def pass_last(half):
        for which, step in ((0, 1), (1, -1)):
            copies.wait_recv(near_last.at[half, which], ("nl", half, which))
            ref = block(half, 0, step, which)
            ref[...] = (ref[...].astype(F32) + near_last[half, which].astype(F32)).astype(BF16)
            send(block(half, 0, step), whole_last.at[half, which], ("wl", half, which), half, 1, step)

    def total(half):
        for which in (0, 1):
            copies.wait_recv(whole_last.at[half, which], ("wl", half, which))
        return (
            block(half, 0, 0)[...].astype(F32)
            + whole_last[half, 0].astype(F32)
            + whole_last[half, 1].astype(F32)
        )

    return far, pass_on, settle, far_last, pass_last, total


def update_kernel(
    rail_ref, back_ref, next_ref, gain_ref, mg_ref, mu_ref, og_ref, ou_ref, sg_ref, su_ref,
    result_ref, out_ref, nmg_ref, nmu_ref, nog_ref, nou_ref, nsg_ref, nsu_ref, scale_ref,
    weights, rail, near, whole, near_last, whole_last, spread, gather, next_pad, block_ref, flat_ref,
    state, updates, gate_sum, up_sum, send_sem, recv_sem, local_sem, state_sem,
):
    y, x, core = coords()
    hidden = out_ref.shape[1]
    features = next_ref.shape[1]
    copies = Copies(send_sem, recv_sem)
    fetch = pltpu.make_async_copy(rail_ref, rail, local_sem)
    fetch.start()
    loads = [
        pltpu.make_async_copy(ref.at[:, 0, :], state.at[i], state_sem.at[i])
        for i, ref in enumerate((mg_ref, mu_ref, og_ref, ou_ref, sg_ref, su_ref))
    ]
    for load in loads:
        load.start()
    plane_barrier()
    fetch.wait()
    far, pass_on, settle, far_last, pass_last, total = reduce_steps(
        rail, near, whole, near_last, whole_last, copies, hidden
    )
    order = (2, 1, 3, 0)
    for other in order:
        far(0, other)
        far(1, other)
    pad_matrix(spread, 1)
    widened, inverse = rms(next_ref[...])
    next_normed = (widened * inverse * gain_ref[...]).astype(BF16)
    next_pad[...] = mm(next_normed, spread[...]).astype(BF16)
    pad_matrix(gather, 0)
    result_ref[...] = mm(back_ref[...], gather[...]).astype(BF16)
    for other in order:
        pass_on(0, other)
        pass_on(1, other)
    for other in order:
        settle(0, other)
        settle(1, other)
        if other == 2:
            far_last(0)
            far_last(1)
    pass_last(0)
    pass_last(1)

    begin, rounds, from_sibling = gather_steps(weights, copies, hidden)
    lanes = flat_ref.shape[1]
    lines = hidden // lanes
    mine = pl.multiple_of(lax.axis_index("dp") * PAD, PAD)
    for load in loads:
        load.wait()
    stores = []
    for half, outs in ((0, (nmg_ref, nog_ref, nsg_ref)), (1, (nmu_ref, nou_ref, nsu_ref))):
        gradient = total(half)
        for line in range(lines):
            flat_ref[pl.ds(line, ROWS, stride=lines), :] = gradient[:ROWS, line * lanes : (line + 1) * lanes]
        gradient = flat_ref[...]
        results = adam_update(state[half], state[2 + half], state[4 + half], gradient)
        for i, value in enumerate(results):
            number = 2 * i + half
            updates[number] = value
            stores.append(
                pltpu.make_async_copy(updates.at[number], outs[i].at[:, 0, :], state_sem.at[number])
            )
            stores[-1].start()
        updated = results[0]
        peak = jnp.max(jnp.abs(updated), keepdims=True)
        high = peak.astype(BF16).astype(F32)
        middle = (peak - high).astype(BF16).astype(F32)
        low = peak - high - middle
        tail = lax.broadcasted_iota(jnp.int32, (PAD - ROWS, hidden), 0)
        for line in range(lines):
            block_ref[pl.ds(0, ROWS), pl.ds(line * lanes, lanes)] = updates[half, pl.ds(line, ROWS, stride=lines), :]
        block_ref[pl.ds(ROWS, PAD - ROWS), :] = jnp.where(
            tail == 0, high, jnp.where(tail == 1, middle, jnp.where(tail == 2, low, 0.0))
        )
        weights[pl.ds(mine, PAD), pl.ds(half * hidden, hidden)] = block_ref[...].astype(BF16)
        begin(half)
    width = next_pad.shape[1] // RING

    def line_of(half, step, cols):
        rows = pl.ds(pl.multiple_of(((y + step) % RING) * width, width), width)
        return mm(next_pad[:, rows], weights[rows, pl.ds(half * hidden + cols.start, cols.size)])

    def line_ready(half, step):
        for i in range(RING):
            from_sibling(half, *((i, step) if half == 0 else (step, i)))

    def add_line(half, step, target, fresh):
        line_ready(half, step)
        for piece in tiles(hidden):
            cols = pl.ds(*piece)
            product = line_of(half, step, cols)
            target[:, cols] = product if fresh else target[:, cols] + product

    after = {
        2: lambda: add_line(0, 0, gate_sum, True),
        4: lambda: add_line(1, 0, up_sum, True),
        6: lambda: add_line(1, 3, up_sum, False),
        8: lambda: add_line(1, 1, up_sum, False),
    }
    for number, items in enumerate(rounds):
        for item in items:
            item()
        if number in after:
            after[number]()
    for step in (3, 1, 2):
        line_ready(0, step)
    line_ready(1, 2)

    peaks = []
    for half in (0, 1):
        heads = weights[:, pl.ds(half * hidden, 128)].astype(F32)
        heads = heads.reshape(heads.shape[0] // PAD, PAD, 128)[:, PAD - 8 :, :]
        level = lax.broadcasted_iota(jnp.int32, heads.shape, 1)
        found = jnp.sum(jnp.where(level >= 4, heads, 0.0), axis=1)
        peaks.append(jnp.max(found, keepdims=True) + scale_eps)
    lane = lax.broadcasted_iota(jnp.int32, scale_ref.shape, 1)
    scale_ref[...] = jnp.where(lane == 0, peaks[0], peaks[1])
    for start, size in tiles(hidden):
        cols = pl.ds(start, size)
        gate = gate_sum[:, cols]
        for step in (3, 1, 2):
            gate = gate + line_of(0, step, cols)
        up = up_sum[:, cols] + line_of(1, 2, cols)
        out_ref[:, cols] = (gate / (1.0 + jnp.exp(-gate)) * up).astype(BF16)
    for store in stores:
        store.wait()
    copies.wait_sends()


def deliver_kernel(count, *refs):
    sources, targets = refs[:count], refs[count : 2 * count]
    holds, load_sem, store_sem = refs[2 * count : 3 * count - 1], refs[-2], refs[-1]

    def flat(ref):
        return ref.at[:, 0, :] if len(ref.shape) == 3 else ref

    loads = [
        pltpu.make_async_copy(flat(sources[i]), hold, load_sem.at[i]) for i, hold in enumerate(holds)
    ]
    stores = [
        pltpu.make_async_copy(hold, flat(targets[i]), store_sem.at[i]) for i, hold in enumerate(holds)
    ]
    for load in loads:
        load.start()
    targets[-1][...] = sources[-1][...]
    for load, store in zip(loads, stores):
        load.wait()
        store.start()
    for store in stores:
        store.wait()


VMEM = pl.BlockSpec(memory_space=pltpu.VMEM)
SMEM = pl.BlockSpec(memory_space=pltpu.SMEM)
ANY = pl.BlockSpec(memory_space=pl.ANY)
HBM = pl.BlockSpec(memory_space=pltpu.HBM)


def shards(
    section_inputs,
    cotangent,
    norm_gain,
    quant_gate,
    quant_up,
    scales,
    down_proj,
    master_gate,
    master_up,
    moment_gate,
    moment_up,
    second_gate,
    second_up,
    next_inputs,
):
    tokens, features = cotangent.shape
    hidden = quant_gate.shape[2]
    partners = lax.axis_size("dp")
    padded = partners * PAD
    rail_rows = padded // CORES
    dma = pltpu.SemaphoreType.DMA
    back, rail = pl.pallas_call(
        back_kernel,
        out_shape=(
            jax.ShapeDtypeStruct((tokens, padded), BF16),
            jax.ShapeDtypeStruct((rail_rows, 2 * hidden), BF16),
        ),
        in_specs=[VMEM, VMEM, VMEM, VMEM, VMEM, SMEM, ANY],
        out_specs=(VMEM, VMEM),
        scratch_shapes=[
            pltpu.VMEM((padded, 2 * hidden), BF16),
            pltpu.VMEM((2 * hidden, padded), BF16),
            pltpu.VMEM((hidden, features), BF16),
            pltpu.VMEM((padded, hidden), BF16),
            pltpu.VMEM((features, padded), BF16),
            pltpu.VMEM((padded, features), BF16),
            pltpu.VMEM((tokens, padded), BF16),
            pltpu.VMEM((tokens, padded), F32),
            pltpu.VMEM((tokens, 1), F32),
            pltpu.VMEM((1, padded), F32),
            pltpu.VMEM((tokens, hidden), F32),
            pltpu.VMEM((tokens, hidden), F32),
            pltpu.VMEM((tokens, hidden), F32),
            pltpu.VMEM((max(PARTS), hidden), F32),
            pltpu.VMEM((tokens, padded), BF16),
            pltpu.VMEM((2 * tokens, 2 * hidden), BF16),
            pltpu.VMEM((rail_rows, 3 * tokens), BF16),
            pltpu.VMEM((PAD, 2 * hidden), BF16),
            dma((80,)),
            dma((80,)),
            dma((len(PARTS) * RING,)),
            dma((len(PARTS) * RING,)),
            dma(()),
        ],
        compiler_params=pltpu.CompilerParams(
            collective_id=0, has_side_effects=True, vmem_limit_bytes=60 * 2**20
        ),
    )(quant_gate[0], quant_up[0], section_inputs[0], cotangent, norm_gain, scales, down_proj[0])
    lanes = 128
    lines = ROWS * hidden // lanes
    row = jax.ShapeDtypeStruct((lines, 1, lanes), F32)
    flat = [
        value.transpose(1, 0, 2).reshape(row.shape)
        for value in (master_gate, master_up, moment_gate, moment_up, second_gate, second_up)
    ]
    outs = pl.pallas_call(
        update_kernel,
        out_shape=(
            jax.ShapeDtypeStruct((tokens, features), BF16),
            jax.ShapeDtypeStruct((tokens, hidden), BF16),
        )
        + (row,) * 6
        + (jax.ShapeDtypeStruct((1, 2), F32),),
        in_specs=[ANY] + [VMEM] * 3 + [ANY] * 6,
        out_specs=(VMEM,) * 2 + (ANY,) * 6 + (VMEM,),
        scratch_shapes=[
            pltpu.VMEM((padded, 2 * hidden), BF16),
            pltpu.VMEM((rail_rows, 2 * hidden), BF16),
            pltpu.VMEM((2, RING, 2, PAD // 2, hidden), BF16),
            pltpu.VMEM((2, RING, 2, PAD, hidden), BF16),
            pltpu.VMEM((2, 2, PAD // 2, hidden), BF16),
            pltpu.VMEM((2, 2, PAD, hidden), BF16),
            pltpu.VMEM((features, padded), BF16),
            pltpu.VMEM((padded, features), BF16),
            pltpu.VMEM((tokens, padded), BF16),
            pltpu.VMEM((PAD, hidden), F32),
            pltpu.VMEM((lines, lanes), F32),
            pltpu.VMEM((6, lines, lanes), F32),
            pltpu.VMEM((6, lines, lanes), F32),
            pltpu.VMEM((tokens, hidden), F32),
            pltpu.VMEM((tokens, hidden), F32),
            dma((128,)),
            dma((128,)),
            dma(()),
            dma((6,)),
        ],
        compiler_params=pltpu.CompilerParams(
            collective_id=1, has_side_effects=True, vmem_limit_bytes=60 * 2**20
        ),
    )(rail, back, next_inputs[0], norm_gain, *flat)
    outs = pl.pallas_call(
        functools.partial(deliver_kernel, len(outs)),
        out_shape=tuple(jax.ShapeDtypeStruct(value.shape, value.dtype) for value in outs),
        in_specs=[HBM] * 8 + [VMEM],
        out_specs=(HBM,) * 8 + (VMEM,),
        scratch_shapes=[
            pltpu.VMEM((value.shape[0], value.shape[-1]), value.dtype) for value in outs[:-1]
        ]
        + [dma((8,)), dma((8,))],
        compiler_params=pltpu.CompilerParams(vmem_limit_bytes=60 * 2**20),
    )(*outs)
    result, next_hidden = outs[:2]
    return (
        (result[None],)
        + tuple(value.reshape(ROWS, 1, hidden).transpose(1, 0, 2) for value in outs[2:8])
        + (outs[8], next_hidden[None])
    )


def solution(mesh):
    placed = (
        P("section", "dp", None),
        P("dp", None),
        P("section", None),
        P("section", "dp", None),
        P("section", "dp", None),
        P("section", None),
        P("section", None, None),
        P("section", "dp", None),
        P("section", "dp", None),
        P("section", "dp", None),
        P("section", "dp", None),
        P("section", "dp", None),
        P("section", "dp", None),
        P("section", "dp", None),
    )
    return jax.shard_map(
        shards,
        mesh=mesh,
        in_specs=placed,
        out_specs=(
            P("section", "dp", None),
            P("section", "dp", None),
            P("section", "dp", None),
            P("section", "dp", None),
            P("section", "dp", None),
            P("section", "dp", None),
            P("section", "dp", None),
            P("section", None),
            P("section", "dp", None),
        ),
        check_vma=False,
    )
```

```python
import functools
import jax
import jax.numpy as jnp
from jax import lax
from jax.experimental import pallas as pl
from jax.experimental.pallas import tpu as pltpu
from jax.sharding import PartitionSpec as P

beta_one = 0.9
beta_two = 0.95
learn_rate = 0.002
decay_rate = 0.1
adam_steps = 100.0
norm_eps = 1e-06
adam_eps = 1e-08
scale_eps = 1e-06

RING = 4
CORES = 2
ROWS = 28
PAD = 32
KEEP = 1920
PARTS = (64, 64, 64, 64)
F32 = jnp.float32
BF16 = jnp.bfloat16
NT = (((1,), (1,)), ((), ()))
NN = (((1,), (0,)), ((), ()))


def mm(a, b, dims=NN):
    return lax.dot_general(a, b, dims, preferred_element_type=F32)


def tiles(count, step=512):
    return [(i, min(step, count - i)) for i in range(0, count, step)]


def coords():
    dp = lax.axis_index("dp")
    chip = dp // CORES
    return chip // RING, chip % RING, dp % CORES


def dp_index(y, x, core):
    return (y * RING + x) * CORES + core


class Copies:
    def __init__(self, send_sem, recv_sem):
        self.send_sem, self.recv_sem = send_sem, recv_sem
        self.sent = []
        self.slots = {}

    def slot(self, key):
        return self.slots.setdefault(key, len(self.slots))

    def start(self, src, dst, key, device):
        copy = pltpu.make_async_remote_copy(
            src_ref=src,
            dst_ref=dst,
            send_sem=self.send_sem.at[len(self.sent)],
            recv_sem=self.recv_sem.at[self.slot(key)],
            device_id={"dp": device},
            device_id_type=pl.DeviceIdType.MESH,
        )
        copy.start()
        self.sent.append(copy)

    def wait_recv(self, dst, key):
        pltpu.make_async_remote_copy(
            src_ref=dst,
            dst_ref=dst,
            send_sem=self.send_sem.at[0],
            recv_sem=self.recv_sem.at[self.slot(key)],
            device_id={"dp": lax.axis_index("dp")},
            device_id_type=pl.DeviceIdType.MESH,
        ).wait_recv()

    def wait_sends(self):
        for copy in self.sent:
            copy.wait_send()


def plane_barrier(extra=()):
    y, x, core = coords()
    sem = pltpu.get_barrier_semaphore()
    for device in (
        dp_index((y + 1) % RING, x, core),
        dp_index((y + RING - 1) % RING, x, core),
        dp_index(y, (x + 1) % RING, core),
        dp_index(y, (x + RING - 1) % RING, core),
        dp_index(y, x, 1 - core),
    ):
        pl.semaphore_signal(sem, inc=1, device_id={"dp": device}, device_id_type=pl.DeviceIdType.MESH)
    for section in extra:
        pl.semaphore_signal(sem, inc=1, device_id={"section": section}, device_id_type=pl.DeviceIdType.MESH)
    pl.semaphore_wait(sem, 5 + len(extra))


def part_of(ref, row, col, which, hidden):
    row = pl.multiple_of(row + which * (PAD // 2), PAD // 2)
    return ref.at[pl.ds(row, PAD // 2), pl.ds(col, KEEP if which else hidden)]


def pack(ref, row, col, hidden):
    extra = hidden - KEEP
    rows = pl.ds(pl.multiple_of(row + PAD // 2, PAD // 2), PAD // 2)
    source = ref[rows, pl.ds(col + KEEP, extra)].astype(F32)
    number = lax.broadcasted_iota(jnp.int32, source.shape, 0)
    for i in range(3):
        cols = pl.ds(col + i * extra, extra)
        moved = pltpu.roll(source, 12 - 4 * i, 0)
        ref[rows, cols] = jnp.where(number >= 12, moved, ref[rows, cols].astype(F32)).astype(ref.dtype)


def last_columns(lower, extra):
    number = lax.broadcasted_iota(jnp.int32, (lower.shape[0], extra), 0)
    result = jnp.zeros((lower.shape[0], extra), F32)
    for i in range(3):
        moved = pltpu.roll(lower[:, i * extra : (i + 1) * extra], 4 + 4 * i, 0)
        result = jnp.where(number // 4 == i, moved, result)
    return result


def unpack(ref, row, col, hidden):
    extra = hidden - KEEP
    rows = pl.ds(pl.multiple_of(row + PAD // 2, PAD // 2), PAD // 2)
    lower = ref[rows, pl.ds(col, 3 * extra)].astype(F32)
    ref[rows, pl.ds(col + KEEP, extra)] = last_columns(lower, extra).astype(BF16)


def gather_steps(buf, copies, hidden):
    y, x, core = coords()

    def place(half, first, second):
        if half == 0:
            return (y + second) % RING, (x + first) % RING
        return (y + first) % RING, (x + second) % RING

    def piece(half, first, second, which, owner_core=None):
        py, px = place(half, first, second)
        base = dp_index(py, px, core if owner_core is None else owner_core) * PAD
        return part_of(buf, base, half * hidden, which, hidden)

    def send(half, first, second, which, axis, step):
        if axis == 0:
            py, px = place(half, step, 0)
            key = ("ag", half, (first - step) % RING, second, which)
        else:
            py, px = place(half, 0, step)
            key = ("ag", half, first, (second - step) % RING, which)
        ref = piece(half, first, second, which)
        copies.start(ref, ref, key, dp_index(py, px, core))

    def sibling(half, first, second):
        for which in (0, 1):
            ref = piece(half, first, second, which)
            copies.start(ref, ref, ("sib", half, first, second, which), dp_index(y, x, 1 - core))

    def landed(half, first, second, which):
        copies.wait_recv(piece(half, first, second, which), ("ag", half, first, second, which))

    def arrive(half, first, second):
        landed(half, first, second, 0)
        landed(half, first, second, 1)

    def both_ways(half, first, axis):
        for which in (0, 1):
            send(half, first, 0, which, axis, 1)
            send(half, first, 0, which, axis, -1)

    def bulk(half, first):
        both_ways(half, first, 1)

    def relay(half, first, second):
        axis = 0 if second == 0 else 1
        step = 1 if (first, second)[axis] == 3 else -1
        which = 0 if step == 1 else 1
        if axis == 1 and first in (1, 2):
            which = 1 - which
        landed(half, first, second, which)
        send(half, first, second, which, axis, step)
        landed(half, first, second, 1 - which)

    def begin(half):
        both_ways(half, 0, 0)
        bulk(half, 0)
        sibling(half, 0, 0)

    def group(*steps):
        return [functools.partial(step, half, *key) for step, *key in steps for half in (0, 1)]

    def lines(first, *more):
        return group(
            (relay, first, 3), (relay, first, 1), *more, (sibling, first, 3), (sibling, first, 1)
        )

    def opposite(first, second):
        return group((arrive, first, second), (sibling, first, second))

    rounds = (
        group((relay, 3, 0), (relay, 1, 0), (bulk, 3), (sibling, 3, 0), (sibling, 1, 0)),
        lines(0, (bulk, 1)),
        opposite(2, 0),
        lines(3, (bulk, 2)),
        opposite(0, 2),
        lines(1),
        opposite(3, 2),
        lines(2),
        opposite(1, 2),
        opposite(2, 2),
    )

    def from_sibling(half, first, second):
        for which in (0, 1):
            copies.wait_recv(
                piece(half, first, second, which, 1 - core), ("sib", half, first, second, which)
            )

    return begin, rounds, from_sibling


def pad_matrix(ref, padded_axis):
    chunk = 128
    for start in range(0, ref.shape[0], chunk):
        shape = (chunk, ref.shape[1])
        ids = [lax.broadcasted_iota(jnp.int32, shape, axis) for axis in (0, 1)]
        ids[0] = ids[0] + start
        plain, number = ids[1 - padded_axis], ids[padded_axis]
        block, inner = number // PAD, number % PAD
        hit = jnp.logical_and(inner < ROWS, block * ROWS + inner == plain)
        ref[pl.ds(start, chunk), :] = jnp.where(hit, 1.0, 0.0).astype(BF16)


def rms(inputs):
    widened = inputs.astype(F32)
    return widened, lax.rsqrt(jnp.mean(widened * widened, axis=-1, keepdims=True) + norm_eps)


def back_kernel(
    gate_ref, up_ref, x_ref, cot_ref, gain_ref, scale_ref, down_ref,
    outgoing, rail_ref,
    weights, turned, down_raw, down_turned, spread, gather, normed_pad, wide_pad, inv_ref, gain_pad,
    slope_gate, slope_up, slope_sum, partial, upstream, grads, sides, block,
    send_sem, recv_sem, wave_send, wave_recv, local_sem,
):
    y, x, core = coords()
    section = lax.axis_index("section")
    sections = lax.axis_size("section")
    last = sections - 1
    tokens, features = x_ref.shape
    hidden = down_ref.shape[0]
    padded = gather.shape[0]
    rail = padded // CORES
    width = padded // RING
    copies = Copies(send_sem, recv_sem)
    fetch = pltpu.make_async_copy(down_ref, down_raw, local_sem)
    fetch.start()
    mine = pl.multiple_of(lax.axis_index("dp") * PAD, PAD)
    block[...] = jnp.zeros(block.shape, BF16)
    block[pl.ds(0, ROWS), pl.ds(0, hidden)] = gate_ref[...]
    block[pl.ds(0, ROWS), pl.ds(hidden, hidden)] = up_ref[...]
    pack(block, 0, 0, hidden)
    pack(block, 0, hidden, hidden)
    weights[pl.ds(mine, PAD), :] = block[...]
    plane_barrier(((section + 1) % sections, (section + sections - 1) % sections))
    begin, rounds, from_sibling = gather_steps(weights, copies, hidden)
    begin(0)
    begin(1)

    pad_matrix(spread, 1)
    one_hot = spread[...]
    widened, inverse = rms(x_ref[...])
    gain = gain_ref[...]
    normed = (widened * inverse * gain).astype(BF16)
    inv_ref[...] = inverse
    high = gain.astype(BF16)
    rest = gain - high.astype(F32)
    middle = rest.astype(BF16)
    low = (rest - middle.astype(F32)).astype(BF16)
    gain_pad[...] = mm(high, one_hot) + mm(middle, one_hot) + mm(low, one_hot)
    wide_pad[...] = mm(x_ref[...], one_hot)
    normed_pad[...] = mm(normed, one_hot).astype(BF16)

    flat = normed_pad[...].T.reshape(padded // (CORES * PAD), CORES, PAD, tokens)
    even = flat[:, 0].reshape(rail, tokens)
    odd = flat[:, 1].reshape(rail, tokens)
    sides[:, pl.ds(0, tokens)] = jnp.where(core == 0, even, odd)
    sides[:, pl.ds(2 * tokens, tokens)] = jnp.where(core == 0, odd, even)
    other = dp_index(y, x, 1 - core)
    copies.start(
        sides.at[:, pl.ds(2 * tokens, tokens)], sides.at[:, pl.ds(tokens, tokens)], "side", other
    )

    def down_piece(start, size):
        down_turned[:, pl.ds(start, size)] = mm(
            gather[...], down_raw[pl.ds(start, size), :], NT
        ).astype(BF16)

    def weight_rows(half, step):
        for i in range(RING):
            from_sibling(half, *((i, step) if half == 0 else (step, i)))
        rows = pl.ds(pl.multiple_of(((y + step) % RING) * width, width), width)
        for number in range(width // PAD):
            unpack(weights, ((y + step) % RING) * width + number * PAD, half * hidden, hidden)
        target = (slope_gate, slope_up)[half]
        left = normed_pad[:, rows]
        for start, size in tiles(hidden):
            here = weights[rows, pl.ds(half * hidden + start, size)]
            turned[pl.ds(half * hidden + start, size), rows] = here.T
            product = mm(left, here)
            cols = pl.ds(start, size)
            target[:, cols] = product if step == 0 else target[:, cols] + product

    downs = [functools.partial(down_piece, *piece) for piece in tiles(hidden, 256)]

    def run(items, count=0):
        for item in items:
            item()
        for _ in range(count):
            downs.pop(0)()

    run(rounds[0])
    pad_matrix(gather, 0)
    fetch.wait()

    @pl.when(section == last)
    def _():
        upstream[...] = mm(cot_ref[...], one_hot).astype(BF16)

    run(rounds[1], 2)
    run(rounds[2])
    weight_rows(0, 0)
    run(rounds[3], 3)
    run(rounds[4])
    weight_rows(1, 0)
    run(rounds[5], 3)
    run(rounds[6])
    weight_rows(1, 3)
    run(rounds[7], len(downs))
    run(rounds[8])
    weight_rows(1, 1)
    run(rounds[9])
    weight_rows(0, 3)
    weight_rows(0, 1)
    weight_rows(0, 2)
    weight_rows(1, 2)

    parts = []
    for size in PARTS:
        parts.append((sum(PARTS[: len(parts)]), size))

    def slopes(first, count):
        rows = pl.ds(first, count)
        for start, size in tiles(hidden):
            cols = pl.ds(start, size)
            gate = slope_gate[rows, cols] * scale_ref[0, 0]
            up = slope_up[rows, cols] * scale_ref[0, 1]
            sigmoid = 1.0 / (1.0 + jnp.exp(-gate))
            by_gate = up * (sigmoid * (1.0 + gate * (1.0 - sigmoid)))
            by_up = gate * sigmoid
            slope_gate[rows, cols] = by_gate
            slope_up[rows, cols] = by_up
            slope_sum[rows, cols] = by_gate * gate + by_up * up

    slopes(*parts[0])

    @pl.when(section < last)
    def _():
        slopes(parts[1][0], tokens - parts[1][0])

    def wave_copy(part, piece):
        rows, cols = pl.ds(*parts[part]), pl.ds(piece * width, width)
        return pltpu.make_async_remote_copy(
            src_ref=outgoing.at[rows, cols],
            dst_ref=upstream.at[rows, cols],
            send_sem=wave_send.at[part * RING + piece],
            recv_sem=wave_recv.at[part * RING + piece],
            device_id={"section": jnp.maximum(section - 1, 0)},
            device_id_type=pl.DeviceIdType.MESH,
        )

    for part, (first, count) in enumerate(parts):
        rows = pl.ds(first, count)
        if part > 0:

            @pl.when(section == last)
            def _():
                slopes(first, count)

        sums = jnp.zeros((count, 128), F32)
        for piece in range(RING):
            span = pl.ds(piece * width, width)

            @pl.when(section < last)
            def _():
                wave_copy(part, piece).wait_recv()

            left = upstream[rows, span]
            for start, size in tiles(hidden):
                cols = pl.ds(start, size)
                product = mm(left, down_turned[span, cols])
                if piece > 0:
                    product = product + partial[pl.ds(0, count), cols]
                if piece < RING - 1:
                    partial[pl.ds(0, count), cols] = product
                    continue
                grads[rows, cols] = (product * slope_gate[rows, cols]).astype(BF16)
                grads[rows, pl.ds(hidden + start, size)] = (product * slope_up[rows, cols]).astype(BF16)
                product = product * slope_sum[rows, cols]
                for lane in range(0, size, 128):
                    sums = sums + product[:, lane : lane + 128]
        copies.start(grads.at[rows], grads.at[pl.ds(tokens + first, count)], ("grads", part), other)
        inverse = inv_ref[rows, :]
        mean = jnp.sum(sums, axis=-1, keepdims=True) * (inverse * inverse / features)
        for piece in range(RING):
            span = pl.ds(piece * width, width)
            normed_grad = (
                mm(grads[rows, pl.ds(0, hidden)], turned[pl.ds(0, hidden), span]) * scale_ref[0, 0]
                + mm(grads[rows, pl.ds(hidden, hidden)], turned[pl.ds(hidden, hidden), span])
                * scale_ref[0, 1]
            )
            outgoing[rows, span] = (
                upstream[rows, span].astype(F32)
                + inverse * (gain_pad[:, span] * normed_grad)
                - wide_pad[rows, span] * mean
            ).astype(BF16)

            @pl.when(section > 0)
            def _():
                wave_copy(part, piece).start()

    copies.wait_recv(sides.at[:, pl.ds(tokens, tokens)], "side")
    for part, (first, count) in enumerate(parts):
        copies.wait_recv(grads.at[pl.ds(tokens + first, count)], ("grads", part))
    both = sides[:, pl.ds(0, 2 * tokens)]
    for start, size in tiles(2 * hidden):
        cols = pl.ds(start, size)
        rail_ref[:, cols] = mm(both, grads[:, cols]).astype(BF16)

    @pl.when(section > 0)
    def _():
        for part in range(len(parts)):
            for piece in range(RING):
                wave_copy(part, piece).wait_send()

    copies.wait_sends()


def adam_update(master, moment_old, second_old, gradient):
    moment_one = beta_one * moment_old + (1.0 - beta_one) * gradient
    moment_two = beta_two * second_old + (1.0 - beta_two) * gradient * gradient
    unbiased_one = moment_one / (1.0 - beta_one**adam_steps)
    unbiased_two = moment_two / (1.0 - beta_two**adam_steps)
    updated = master - learn_rate * (
        unbiased_one / (jnp.sqrt(unbiased_two) + adam_eps) + decay_rate * master
    )
    return (updated, moment_one, moment_two)


def reduce_steps(rail, near, whole, near_last, whole_last, copies, hidden):
    y, x, core = coords()

    def place(half, bulk, other):
        if half == 0:
            return (y + bulk) % RING, (x + other) % RING
        return (y + other) % RING, (x + bulk) % RING

    def block(half, bulk, other, which):
        py, px = place(half, bulk, other)
        return part_of(rail, (py * RING + px) * PAD, half * hidden, which, hidden)

    def send(src, dst, key, half, axis, step):
        py, px = place(half, step, 0) if axis == 0 else place(half, 0, step)
        copies.start(src, dst, key, dp_index(py, px, core))

    def ways(other):
        return ((0, 1), (1, -1)) if other in (0, 3) else ((1, 1), (0, -1))

    def trim(ref, which):
        return part_of(ref, 0, 0, which, hidden)

    def narrow(ref, which):
        return ref.at[:, pl.ds(0, KEEP)] if which else ref

    def far(half, other):
        for which, step in ways(other):
            send(block(half, 2, other, which), narrow(near.at[half, other, which], which), ("n", half, other, which), half, 0, step)

    def pass_on(half, other):
        for which, step in ways(other):
            here = narrow(near.at[half, other, which], which)
            copies.wait_recv(here, ("n", half, other, which))
            ref = block(half, step, other, which)
            ref[...] = (ref[...].astype(F32) + here[...].astype(F32)).astype(BF16)
            side = 0 if step == 1 else 1
            for part in (0, 1):
                send(block(half, step, other, part), trim(whole.at[half, other, side], part), ("w", half, other, side, part), half, 0, step)

    def settle(half, other):
        for part in (0, 1):
            ref = block(half, 0, other, part)
            value = ref[...].astype(F32)
            for side in (0, 1):
                here = trim(whole.at[half, other, side], part)
                copies.wait_recv(here, ("w", half, other, side, part))
                value = value + here[...].astype(F32)
            ref[...] = value.astype(BF16)

    def far_last(half):
        for which, step in ways(0):
            send(block(half, 0, 2, which), narrow(near_last.at[half, which], which), ("nl", half, which), half, 1, step)

    def pass_last(half):
        for which, step in ways(0):
            here = narrow(near_last.at[half, which], which)
            copies.wait_recv(here, ("nl", half, which))
            ref = block(half, 0, step, which)
            ref[...] = (ref[...].astype(F32) + here[...].astype(F32)).astype(BF16)
            side = 0 if step == 1 else 1
            for part in (0, 1):
                send(block(half, 0, step, part), trim(whole_last.at[half, side], part), ("wl", half, side, part), half, 1, step)

    def total(half):
        sums = []
        for part in (0, 1):
            value = block(half, 0, 0, part)[...].astype(F32)
            for side in (0, 1):
                here = trim(whole_last.at[half, side], part)
                copies.wait_recv(here, ("wl", half, side, part))
                value = value + here[...].astype(F32)
            sums.append(value)
        return sums

    return far, pass_on, settle, far_last, pass_last, total


def update_kernel(
    rail_ref, back_ref, next_ref, gain_ref, mg_ref, mu_ref, og_ref, ou_ref, sg_ref, su_ref,
    result_ref, out_ref, nmg_ref, nmu_ref, nog_ref, nou_ref, nsg_ref, nsu_ref, scale_ref,
    weights, rail, near, whole, near_last, whole_last, spread, gather, next_pad, block_ref, flat_ref,
    state, updates, gate_sum, up_sum, send_sem, recv_sem, local_sem, state_sem,
):
    y, x, core = coords()
    hidden = out_ref.shape[1]
    features = next_ref.shape[1]
    copies = Copies(send_sem, recv_sem)
    fetch = pltpu.make_async_copy(rail_ref, rail, local_sem)
    fetch.start()
    loads = [
        pltpu.make_async_copy(ref.at[:, 0, :], state.at[i], state_sem.at[i])
        for i, ref in enumerate((mg_ref, mu_ref, og_ref, ou_ref, sg_ref, su_ref))
    ]
    for load in loads:
        load.start()
    plane_barrier()
    fetch.wait()
    for number in range(rail.shape[0] // PAD):
        pack(rail, number * PAD, 0, hidden)
        pack(rail, number * PAD, hidden, hidden)
    far, pass_on, settle, far_last, pass_last, total = reduce_steps(
        rail, near, whole, near_last, whole_last, copies, hidden
    )
    order = (2, 1, 3, 0)
    for other in order:
        far(0, other)
        far(1, other)
    pad_matrix(spread, 1)
    widened, inverse = rms(next_ref[...])
    next_normed = (widened * inverse * gain_ref[...]).astype(BF16)
    next_pad[...] = mm(next_normed, spread[...]).astype(BF16)
    pad_matrix(gather, 0)
    result_ref[...] = mm(back_ref[...], gather[...]).astype(BF16)
    for other in order:
        pass_on(0, other)
        pass_on(1, other)
    for other in order:
        settle(0, other)
        settle(1, other)
        if other == 2:
            far_last(0)
            far_last(1)
    pass_last(0)
    pass_last(1)

    begin, rounds, from_sibling = gather_steps(weights, copies, hidden)
    lanes = flat_ref.shape[1]
    lines = hidden // lanes
    mine = pl.multiple_of(lax.axis_index("dp") * PAD, PAD)
    for load in loads:
        load.wait()
    stores = []
    for half, outs in ((0, (nmg_ref, nog_ref, nsg_ref)), (1, (nmu_ref, nou_ref, nsu_ref))):
        upper, lower = total(half)
        lower = jnp.concatenate([lower, last_columns(lower, hidden - KEEP)], axis=1)
        for line in range(lines):
            span = slice(line * lanes, (line + 1) * lanes)
            flat_ref[pl.ds(line, PAD // 2, stride=lines), :] = upper[:, span]
            flat_ref[pl.ds(PAD // 2 * lines + line, ROWS - PAD // 2, stride=lines), :] = lower[
                : ROWS - PAD // 2, span
            ]
        gradient = flat_ref[...]
        results = adam_update(state[half], state[2 + half], state[4 + half], gradient)
        for i, value in enumerate(results):
            number = 2 * i + half
            updates[number] = value
            stores.append(
                pltpu.make_async_copy(updates.at[number], outs[i].at[:, 0, :], state_sem.at[number])
            )
            stores[-1].start()
        updated = results[0]
        peak = jnp.max(jnp.abs(updated), keepdims=True)
        high = peak.astype(BF16).astype(F32)
        middle = (peak - high).astype(BF16).astype(F32)
        low = peak - high - middle
        tail = lax.broadcasted_iota(jnp.int32, (PAD - ROWS, hidden), 0)
        for line in range(lines):
            block_ref[pl.ds(0, ROWS), pl.ds(line * lanes, lanes)] = updates[half, pl.ds(line, ROWS, stride=lines), :]
        block_ref[pl.ds(ROWS, PAD - ROWS), :] = jnp.where(
            tail == 0, high, jnp.where(tail == 1, middle, jnp.where(tail == 2, low, 0.0))
        )
        pack(block_ref, 0, 0, hidden)
        weights[pl.ds(mine, PAD), pl.ds(half * hidden, hidden)] = block_ref[...].astype(BF16)
        begin(half)
    width = next_pad.shape[1] // RING

    def line_of(half, step, cols):
        rows = pl.ds(pl.multiple_of(((y + step) % RING) * width, width), width)
        return mm(next_pad[:, rows], weights[rows, pl.ds(half * hidden + cols.start, cols.size)])

    def line_ready(half, step):
        for i in range(RING):
            from_sibling(half, *((i, step) if half == 0 else (step, i)))
        for number in range(width // PAD):
            unpack(weights, ((y + step) % RING) * width + number * PAD, half * hidden, hidden)

    def add_line(half, step, target, fresh):
        line_ready(half, step)
        for piece in tiles(hidden):
            cols = pl.ds(*piece)
            product = line_of(half, step, cols)
            target[:, cols] = product if fresh else target[:, cols] + product

    after = {
        2: lambda: add_line(0, 0, gate_sum, True),
        4: lambda: add_line(1, 0, up_sum, True),
        6: lambda: add_line(1, 3, up_sum, False),
        8: lambda: add_line(1, 1, up_sum, False),
    }
    for number, items in enumerate(rounds):
        for item in items:
            item()
        if number in after:
            after[number]()
    for step in (3, 1, 2):
        line_ready(0, step)
    line_ready(1, 2)

    peaks = []
    for half in (0, 1):
        heads = weights[:, pl.ds(half * hidden + 3 * (hidden - KEEP), 128)].astype(F32)
        heads = heads.reshape(heads.shape[0] // PAD, PAD, 128)[:, PAD - 8 :, :]
        level = lax.broadcasted_iota(jnp.int32, heads.shape, 1)
        found = jnp.sum(jnp.where(level >= 4, heads, 0.0), axis=1)
        peaks.append(jnp.max(found, keepdims=True) + scale_eps)
    lane = lax.broadcasted_iota(jnp.int32, scale_ref.shape, 1)
    scale_ref[...] = jnp.where(lane == 0, peaks[0], peaks[1])
    for start, size in tiles(hidden):
        cols = pl.ds(start, size)
        gate = gate_sum[:, cols]
        for step in (3, 1, 2):
            gate = gate + line_of(0, step, cols)
        up = up_sum[:, cols] + line_of(1, 2, cols)
        out_ref[:, cols] = (gate / (1.0 + jnp.exp(-gate)) * up).astype(BF16)
    for store in stores:
        store.wait()
    copies.wait_sends()


def deliver_kernel(count, *refs):
    sources, targets = refs[:count], refs[count : 2 * count]
    holds, load_sem, store_sem = refs[2 * count : 3 * count - 1], refs[-2], refs[-1]

    def flat(ref):
        return ref.at[:, 0, :] if len(ref.shape) == 3 else ref

    loads = [
        pltpu.make_async_copy(flat(sources[i]), hold, load_sem.at[i]) for i, hold in enumerate(holds)
    ]
    stores = [
        pltpu.make_async_copy(hold, flat(targets[i]), store_sem.at[i]) for i, hold in enumerate(holds)
    ]
    for load in loads:
        load.start()
    targets[-1][...] = sources[-1][...]
    for load, store in zip(loads, stores):
        load.wait()
        store.start()
    for store in stores:
        store.wait()


VMEM = pl.BlockSpec(memory_space=pltpu.VMEM)
SMEM = pl.BlockSpec(memory_space=pltpu.SMEM)
ANY = pl.BlockSpec(memory_space=pl.ANY)
HBM = pl.BlockSpec(memory_space=pltpu.HBM)


def shards(
    section_inputs,
    cotangent,
    norm_gain,
    quant_gate,
    quant_up,
    scales,
    down_proj,
    master_gate,
    master_up,
    moment_gate,
    moment_up,
    second_gate,
    second_up,
    next_inputs,
):
    tokens, features = cotangent.shape
    hidden = quant_gate.shape[2]
    partners = lax.axis_size("dp")
    padded = partners * PAD
    rail_rows = padded // CORES
    dma = pltpu.SemaphoreType.DMA
    back, rail = pl.pallas_call(
        back_kernel,
        out_shape=(
            jax.ShapeDtypeStruct((tokens, padded), BF16),
            jax.ShapeDtypeStruct((rail_rows, 2 * hidden), BF16),
        ),
        in_specs=[VMEM, VMEM, VMEM, VMEM, VMEM, SMEM, ANY],
        out_specs=(VMEM, VMEM),
        scratch_shapes=[
            pltpu.VMEM((padded, 2 * hidden), BF16),
            pltpu.VMEM((2 * hidden, padded), BF16),
            pltpu.VMEM((hidden, features), BF16),
            pltpu.VMEM((padded, hidden), BF16),
            pltpu.VMEM((features, padded), BF16),
            pltpu.VMEM((padded, features), BF16),
            pltpu.VMEM((tokens, padded), BF16),
            pltpu.VMEM((tokens, padded), F32),
            pltpu.VMEM((tokens, 1), F32),
            pltpu.VMEM((1, padded), F32),
            pltpu.VMEM((tokens, hidden), F32),
            pltpu.VMEM((tokens, hidden), F32),
            pltpu.VMEM((tokens, hidden), F32),
            pltpu.VMEM((max(PARTS), hidden), F32),
            pltpu.VMEM((tokens, padded), BF16),
            pltpu.VMEM((2 * tokens, 2 * hidden), BF16),
            pltpu.VMEM((rail_rows, 3 * tokens), BF16),
            pltpu.VMEM((PAD, 2 * hidden), BF16),
            dma((160,)),
            dma((160,)),
            dma((len(PARTS) * RING,)),
            dma((len(PARTS) * RING,)),
            dma(()),
        ],
        compiler_params=pltpu.CompilerParams(
            collective_id=0, has_side_effects=True, vmem_limit_bytes=60 * 2**20
        ),
    )(quant_gate[0], quant_up[0], section_inputs[0], cotangent, norm_gain, scales, down_proj[0])
    lanes = 128
    lines = ROWS * hidden // lanes
    row = jax.ShapeDtypeStruct((lines, 1, lanes), F32)
    flat = [
        value.transpose(1, 0, 2).reshape(row.shape)
        for value in (master_gate, master_up, moment_gate, moment_up, second_gate, second_up)
    ]
    outs = pl.pallas_call(
        update_kernel,
        out_shape=(
            jax.ShapeDtypeStruct((tokens, features), BF16),
            jax.ShapeDtypeStruct((tokens, hidden), BF16),
        )
        + (row,) * 6
        + (jax.ShapeDtypeStruct((1, 2), F32),),
        in_specs=[ANY] + [VMEM] * 3 + [ANY] * 6,
        out_specs=(VMEM,) * 2 + (ANY,) * 6 + (VMEM,),
        scratch_shapes=[
            pltpu.VMEM((padded, 2 * hidden), BF16),
            pltpu.VMEM((rail_rows, 2 * hidden), BF16),
            pltpu.VMEM((2, RING, 2, PAD // 2, hidden), BF16),
            pltpu.VMEM((2, RING, 2, PAD, hidden), BF16),
            pltpu.VMEM((2, 2, PAD // 2, hidden), BF16),
            pltpu.VMEM((2, 2, PAD, hidden), BF16),
            pltpu.VMEM((features, padded), BF16),
            pltpu.VMEM((padded, features), BF16),
            pltpu.VMEM((tokens, padded), BF16),
            pltpu.VMEM((PAD, hidden), F32),
            pltpu.VMEM((lines, lanes), F32),
            pltpu.VMEM((6, lines, lanes), F32),
            pltpu.VMEM((6, lines, lanes), F32),
            pltpu.VMEM((tokens, hidden), F32),
            pltpu.VMEM((tokens, hidden), F32),
            dma((200,)),
            dma((200,)),
            dma(()),
            dma((6,)),
        ],
        compiler_params=pltpu.CompilerParams(
            collective_id=1, has_side_effects=True, vmem_limit_bytes=60 * 2**20
        ),
    )(rail, back, next_inputs[0], norm_gain, *flat)
    outs = pl.pallas_call(
        functools.partial(deliver_kernel, len(outs)),
        out_shape=tuple(jax.ShapeDtypeStruct(value.shape, value.dtype) for value in outs),
        in_specs=[HBM] * 8 + [VMEM],
        out_specs=(HBM,) * 8 + (VMEM,),
        scratch_shapes=[
            pltpu.VMEM((value.shape[0], value.shape[-1]), value.dtype) for value in outs[:-1]
        ]
        + [dma((8,)), dma((8,))],
        compiler_params=pltpu.CompilerParams(vmem_limit_bytes=60 * 2**20),
    )(*outs)
    result, next_hidden = outs[:2]
    return (
        (result[None],)
        + tuple(value.reshape(ROWS, 1, hidden).transpose(1, 0, 2) for value in outs[2:8])
        + (outs[8], next_hidden[None])
    )


def solution(mesh):
    placed = (
        P("section", "dp", None),
        P("dp", None),
        P("section", None),
        P("section", "dp", None),
        P("section", "dp", None),
        P("section", None),
        P("section", None, None),
        P("section", "dp", None),
        P("section", "dp", None),
        P("section", "dp", None),
        P("section", "dp", None),
        P("section", "dp", None),
        P("section", "dp", None),
        P("section", "dp", None),
    )
    return jax.shard_map(
        shards,
        mesh=mesh,
        in_specs=placed,
        out_specs=(
            P("section", "dp", None),
            P("section", "dp", None),
            P("section", "dp", None),
            P("section", "dp", None),
            P("section", "dp", None),
            P("section", "dp", None),
            P("section", "dp", None),
            P("section", None),
            P("section", "dp", None),
        ),
        check_vma=False,
    )
```

```python
import functools
import jax
import jax.numpy as jnp
from jax import lax
from jax.experimental import pallas as pl
from jax.experimental.pallas import tpu as pltpu
from jax.sharding import PartitionSpec as P

beta_one = 0.9
beta_two = 0.95
learn_rate = 0.002
decay_rate = 0.1
adam_steps = 100.0
norm_eps = 1e-06
adam_eps = 1e-08
scale_eps = 1e-06

RING = 4
CORES = 2
ROWS = 28
PAD = 32
KEEP = 1920
PARTS = (64, 64, 64, 64)
F32 = jnp.float32
BF16 = jnp.bfloat16
NT = (((1,), (1,)), ((), ()))
NN = (((1,), (0,)), ((), ()))


def mm(a, b, dims=NN):
    return lax.dot_general(a, b, dims, preferred_element_type=F32)


def tiles(count, step=512):
    return [(i, min(step, count - i)) for i in range(0, count, step)]


def coords():
    dp = lax.axis_index("dp")
    chip = dp // CORES
    return chip // RING, chip % RING, dp % CORES


def dp_index(y, x, core):
    return (y * RING + x) * CORES + core


class Copies:
    def __init__(self, send_sem, recv_sem):
        self.send_sem, self.recv_sem = send_sem, recv_sem
        self.sent = []
        self.slots = {}

    def slot(self, key):
        return self.slots.setdefault(key, len(self.slots))

    def start(self, src, dst, key, device):
        copy = pltpu.make_async_remote_copy(
            src_ref=src,
            dst_ref=dst,
            send_sem=self.send_sem.at[len(self.sent)],
            recv_sem=self.recv_sem.at[self.slot(key)],
            device_id={"dp": device},
            device_id_type=pl.DeviceIdType.MESH,
        )
        copy.start()
        self.sent.append(copy)

    def wait_recv(self, dst, key):
        pltpu.make_async_remote_copy(
            src_ref=dst,
            dst_ref=dst,
            send_sem=self.send_sem.at[0],
            recv_sem=self.recv_sem.at[self.slot(key)],
            device_id={"dp": lax.axis_index("dp")},
            device_id_type=pl.DeviceIdType.MESH,
        ).wait_recv()

    def wait_sends(self):
        for copy in self.sent:
            copy.wait_send()


def plane_barrier(extra=()):
    y, x, core = coords()
    sem = pltpu.get_barrier_semaphore()
    for device in (
        dp_index((y + 1) % RING, x, core),
        dp_index((y + RING - 1) % RING, x, core),
        dp_index(y, (x + 1) % RING, core),
        dp_index(y, (x + RING - 1) % RING, core),
        dp_index(y, x, 1 - core),
    ):
        pl.semaphore_signal(sem, inc=1, device_id={"dp": device}, device_id_type=pl.DeviceIdType.MESH)
    for section in extra:
        pl.semaphore_signal(sem, inc=1, device_id={"section": section}, device_id_type=pl.DeviceIdType.MESH)
    pl.semaphore_wait(sem, 5 + len(extra))


def part_of(ref, row, col, which, hidden):
    row = pl.multiple_of(row + which * (PAD // 2), PAD // 2)
    return ref.at[pl.ds(row, PAD // 2), pl.ds(col, KEEP if which else hidden)]


def pack(ref, row, col, hidden):
    extra = hidden - KEEP
    rows = pl.ds(pl.multiple_of(row + PAD // 2, PAD // 2), PAD // 2)
    source = ref[rows, pl.ds(col + KEEP, extra)].astype(F32)
    number = lax.broadcasted_iota(jnp.int32, source.shape, 0)
    for i in range(3):
        cols = pl.ds(col + i * extra, extra)
        moved = pltpu.roll(source, 12 - 4 * i, 0)
        ref[rows, cols] = jnp.where(number >= 12, moved, ref[rows, cols].astype(F32)).astype(ref.dtype)


def last_columns(lower, extra):
    number = lax.broadcasted_iota(jnp.int32, (lower.shape[0], extra), 0)
    result = jnp.zeros((lower.shape[0], extra), F32)
    for i in range(3):
        moved = pltpu.roll(lower[:, i * extra : (i + 1) * extra], 4 + 4 * i, 0)
        result = jnp.where(number // 4 == i, moved, result)
    return result


def unpack(ref, row, col, hidden):
    extra = hidden - KEEP
    rows = pl.ds(pl.multiple_of(row + PAD // 2, PAD // 2), PAD // 2)
    lower = ref[rows, pl.ds(col, 3 * extra)].astype(F32)
    ref[rows, pl.ds(col + KEEP, extra)] = last_columns(lower, extra).astype(BF16)


def gather_steps(buf, copies, hidden):
    y, x, core = coords()

    def place(half, first, second):
        if half == 0:
            return (y + second) % RING, (x + first) % RING
        return (y + first) % RING, (x + second) % RING

    def piece(half, first, second, which, owner_core=None):
        py, px = place(half, first, second)
        base = dp_index(py, px, core if owner_core is None else owner_core) * PAD
        return part_of(buf, base, half * hidden, which, hidden)

    def send(half, first, second, which, axis, step):
        if axis == 0:
            py, px = place(half, step, 0)
            key = ("ag", half, (first - step) % RING, second, which)
        else:
            py, px = place(half, 0, step)
            key = ("ag", half, first, (second - step) % RING, which)
        ref = piece(half, first, second, which)
        copies.start(ref, ref, key, dp_index(py, px, core))

    def sibling(half, first, second):
        for which in (0, 1):
            ref = piece(half, first, second, which)
            copies.start(ref, ref, ("sib", half, first, second, which), dp_index(y, x, 1 - core))

    def landed(half, first, second, which):
        copies.wait_recv(piece(half, first, second, which), ("ag", half, first, second, which))

    def arrive(half, first, second):
        landed(half, first, second, 0)
        landed(half, first, second, 1)

    def both_ways(half, first, axis):
        for which in (0, 1):
            send(half, first, 0, which, axis, 1)
            send(half, first, 0, which, axis, -1)

    def bulk(half, first):
        both_ways(half, first, 1)

    def relay(half, first, second):
        axis = 0 if second == 0 else 1
        step = 1 if (first, second)[axis] == 3 else -1
        which = 0 if step == 1 else 1
        if axis == 1 and first in (1, 2):
            which = 1 - which
        landed(half, first, second, which)
        send(half, first, second, which, axis, step)
        landed(half, first, second, 1 - which)

    def begin(half):
        both_ways(half, 0, 0)
        bulk(half, 0)
        sibling(half, 0, 0)

    def group(*steps):
        return [functools.partial(step, half, *key) for step, *key in steps for half in (0, 1)]

    def lines(first, *more):
        return group(
            (relay, first, 3), (relay, first, 1), *more, (sibling, first, 3), (sibling, first, 1)
        )

    def opposite(first, second):
        return group((arrive, first, second), (sibling, first, second))

    rounds = (
        group((relay, 3, 0), (relay, 1, 0), (bulk, 3), (sibling, 3, 0), (sibling, 1, 0)),
        lines(0, (bulk, 1)),
        opposite(2, 0),
        lines(3, (bulk, 2)),
        opposite(0, 2),
        lines(1),
        opposite(3, 2),
        lines(2),
        opposite(1, 2),
        opposite(2, 2),
    )

    def from_sibling(half, first, second):
        for which in (0, 1):
            copies.wait_recv(
                piece(half, first, second, which, 1 - core), ("sib", half, first, second, which)
            )

    return begin, rounds, from_sibling


def pad_matrix(ref, padded_axis):
    chunk = 128
    for start in range(0, ref.shape[0], chunk):
        shape = (chunk, ref.shape[1])
        ids = [lax.broadcasted_iota(jnp.int32, shape, axis) for axis in (0, 1)]
        ids[0] = ids[0] + start
        plain, number = ids[1 - padded_axis], ids[padded_axis]
        block, inner = number // PAD, number % PAD
        hit = jnp.logical_and(inner < ROWS, block * ROWS + inner == plain)
        ref[pl.ds(start, chunk), :] = jnp.where(hit, 1.0, 0.0).astype(BF16)


def rms(inputs):
    widened = inputs.astype(F32)
    return widened, lax.rsqrt(jnp.mean(widened * widened, axis=-1, keepdims=True) + norm_eps)


def back_kernel(
    gate_ref, up_ref, x_ref, cot_ref, gain_ref, scale_ref, down_ref,
    outgoing, rail_ref,
    weights, turned, down_raw, down_turned, spread, gather, normed_pad, wide_pad, inv_ref, gain_pad,
    slope_gate, slope_up, slope_sum, partial, upstream, grads, sides, block, rail_hold,
    send_sem, recv_sem, wave_send, wave_recv, local_sem, rail_sem,
):
    y, x, core = coords()
    section = lax.axis_index("section")
    sections = lax.axis_size("section")
    last = sections - 1
    tokens, features = x_ref.shape
    hidden = down_ref.shape[0]
    padded = gather.shape[0]
    rail = padded // CORES
    width = padded // RING
    copies = Copies(send_sem, recv_sem)
    fetch = pltpu.make_async_copy(down_ref, down_raw, local_sem)
    fetch.start()
    mine = pl.multiple_of(lax.axis_index("dp") * PAD, PAD)
    block[...] = jnp.zeros(block.shape, BF16)
    block[pl.ds(0, ROWS), pl.ds(0, hidden)] = gate_ref[...]
    block[pl.ds(0, ROWS), pl.ds(hidden, hidden)] = up_ref[...]
    pack(block, 0, 0, hidden)
    pack(block, 0, hidden, hidden)
    weights[pl.ds(mine, PAD), :] = block[...]
    plane_barrier(((section + 1) % sections, (section + sections - 1) % sections))
    begin, rounds, from_sibling = gather_steps(weights, copies, hidden)
    begin(0)
    begin(1)

    pad_matrix(spread, 1)
    one_hot = spread[...]
    widened, inverse = rms(x_ref[...])
    gain = gain_ref[...]
    normed = (widened * inverse * gain).astype(BF16)
    inv_ref[...] = inverse
    high = gain.astype(BF16)
    rest = gain - high.astype(F32)
    middle = rest.astype(BF16)
    low = (rest - middle.astype(F32)).astype(BF16)
    gain_pad[...] = mm(high, one_hot) + mm(middle, one_hot) + mm(low, one_hot)
    wide_pad[...] = mm(x_ref[...], one_hot)
    normed_pad[...] = mm(normed, one_hot).astype(BF16)

    flat = normed_pad[...].T.reshape(padded // (CORES * PAD), CORES, PAD, tokens)
    even = flat[:, 0].reshape(rail, tokens)
    odd = flat[:, 1].reshape(rail, tokens)
    sides[:, pl.ds(0, tokens)] = jnp.where(core == 0, even, odd)
    sides[:, pl.ds(2 * tokens, tokens)] = jnp.where(core == 0, odd, even)
    other = dp_index(y, x, 1 - core)
    copies.start(
        sides.at[:, pl.ds(2 * tokens, tokens)], sides.at[:, pl.ds(tokens, tokens)], "side", other
    )

    def down_piece(start, size):
        down_turned[:, pl.ds(start, size)] = mm(
            gather[...], down_raw[pl.ds(start, size), :], NT
        ).astype(BF16)

    def weight_rows(half, step):
        for i in range(RING):
            from_sibling(half, *((i, step) if half == 0 else (step, i)))
        rows = pl.ds(pl.multiple_of(((y + step) % RING) * width, width), width)
        for number in range(width // PAD):
            unpack(weights, ((y + step) % RING) * width + number * PAD, half * hidden, hidden)
        target = (slope_gate, slope_up)[half]
        left = normed_pad[:, rows]
        for start, size in tiles(hidden):
            here = weights[rows, pl.ds(half * hidden + start, size)]
            turned[pl.ds(half * hidden + start, size), rows] = here.T
            product = mm(left, here)
            cols = pl.ds(start, size)
            target[:, cols] = product if step == 0 else target[:, cols] + product

    downs = [functools.partial(down_piece, *piece) for piece in tiles(hidden, 256)]

    def run(items, count=0):
        for item in items:
            item()
        for _ in range(count):
            downs.pop(0)()

    run(rounds[0])
    pad_matrix(gather, 0)
    fetch.wait()

    parts = []
    for size in PARTS:
        parts.append((sum(PARTS[: len(parts)]), size))

    @pl.when(section == last)
    def _():
        outgoing[...] = mm(cot_ref[...], one_hot).astype(BF16)
        for part, place in enumerate(parts):
            for piece in range(RING):
                region = (pl.ds(*place), pl.ds(piece * width, width))
                pltpu.make_async_copy(
                    outgoing.at[region], upstream.at[region], wave_recv.at[part * RING + piece]
                ).start()

    run(rounds[1], 2)
    run(rounds[2])
    weight_rows(0, 0)
    run(rounds[3], 3)
    run(rounds[4])
    weight_rows(1, 0)
    run(rounds[5], 3)
    run(rounds[6])
    weight_rows(1, 3)
    run(rounds[7], len(downs))
    run(rounds[8])
    weight_rows(1, 1)
    run(rounds[9])
    weight_rows(0, 3)
    weight_rows(0, 1)
    weight_rows(0, 2)
    weight_rows(1, 2)

    def slopes(first, count):
        rows = pl.ds(first, count)
        for start, size in tiles(hidden):
            cols = pl.ds(start, size)
            gate = slope_gate[rows, cols] * scale_ref[0, 0]
            up = slope_up[rows, cols] * scale_ref[0, 1]
            sigmoid = 1.0 / (1.0 + jnp.exp(-gate))
            by_gate = up * (sigmoid * (1.0 + gate * (1.0 - sigmoid)))
            by_up = gate * sigmoid
            slope_gate[rows, cols] = by_gate
            slope_up[rows, cols] = by_up
            slope_sum[rows, cols] = by_gate * gate + by_up * up

    slopes(*parts[0])

    @pl.when(section < last)
    def _():
        slopes(parts[1][0], tokens - parts[1][0])

    def wave_copy(part, piece):
        rows, cols = pl.ds(*parts[part]), pl.ds(piece * width, width)
        return pltpu.make_async_remote_copy(
            src_ref=outgoing.at[rows, cols],
            dst_ref=upstream.at[rows, cols],
            send_sem=wave_send.at[part * RING + piece],
            recv_sem=wave_recv.at[part * RING + piece],
            device_id={"section": jnp.maximum(section - 1, 0)},
            device_id_type=pl.DeviceIdType.MESH,
        )

    for part, (first, count) in enumerate(parts):
        rows = pl.ds(first, count)
        if part > 0:

            @pl.when(section == last)
            def _():
                slopes(first, count)

        sums = jnp.zeros((count, 128), F32)
        for piece in range(RING):
            span = pl.ds(piece * width, width)
            wave_copy(part, piece).wait_recv()
            left = upstream[rows, span]
            for start, size in tiles(hidden):
                cols = pl.ds(start, size)
                product = mm(left, down_turned[span, cols])
                if piece > 0:
                    product = product + partial[pl.ds(0, count), cols]
                if piece < RING - 1:
                    partial[pl.ds(0, count), cols] = product
                    continue
                grads[rows, cols] = (product * slope_gate[rows, cols]).astype(BF16)
                grads[rows, pl.ds(hidden + start, size)] = (product * slope_up[rows, cols]).astype(BF16)
                product = product * slope_sum[rows, cols]
                for lane in range(0, size, 128):
                    sums = sums + product[:, lane : lane + 128]
        copies.start(grads.at[rows], grads.at[pl.ds(tokens + first, count)], ("grads", part), other)
        inverse = inv_ref[rows, :]
        mean = jnp.sum(sums, axis=-1, keepdims=True) * (inverse * inverse / features)
        for piece in range(RING):
            span = pl.ds(piece * width, width)
            normed_grad = (
                mm(grads[rows, pl.ds(0, hidden)], turned[pl.ds(0, hidden), span]) * scale_ref[0, 0]
                + mm(grads[rows, pl.ds(hidden, hidden)], turned[pl.ds(hidden, hidden), span])
                * scale_ref[0, 1]
            )
            outgoing[rows, span] = (
                upstream[rows, span].astype(F32)
                + inverse * (gain_pad[:, span] * normed_grad)
                - wide_pad[rows, span] * mean
            ).astype(BF16)

            @pl.when(section > 0)
            def _():
                wave_copy(part, piece).start()

    copies.wait_recv(sides.at[:, pl.ds(tokens, tokens)], "side")
    for part, (first, count) in enumerate(parts):
        copies.wait_recv(grads.at[pl.ds(tokens + first, count)], ("grads", part))
    both = sides[:, pl.ds(0, 2 * tokens)]
    stores = []
    for half in (0, 1):
        for start, size in tiles(hidden):
            cols = pl.ds(half * hidden + start, size)
            rail_hold[:, cols] = mm(both, grads[:, cols]).astype(BF16)
        for number in range(rail // PAD):
            pack(rail_hold, number * PAD, half * hidden, hidden)
        cols = pl.ds(half * hidden, hidden)
        stores.append(
            pltpu.make_async_copy(rail_hold.at[:, cols], rail_ref.at[:, cols], rail_sem.at[half])
        )
        stores[-1].start()

    for store in stores:
        store.wait()

    @pl.when(section > 0)
    def _():
        for part in range(len(parts)):
            for piece in range(RING):
                wave_copy(part, piece).wait_send()

    copies.wait_sends()


def adam_update(master, moment_old, second_old, gradient):
    moment_one = beta_one * moment_old + (1.0 - beta_one) * gradient
    moment_two = beta_two * second_old + (1.0 - beta_two) * gradient * gradient
    unbiased_one = moment_one / (1.0 - beta_one**adam_steps)
    unbiased_two = moment_two / (1.0 - beta_two**adam_steps)
    updated = master - learn_rate * (
        unbiased_one / (jnp.sqrt(unbiased_two) + adam_eps) + decay_rate * master
    )
    return (updated, moment_one, moment_two)


def reduce_steps(rail_ref, rail, near, whole, near_last, whole_last, copies, hidden):
    y, x, core = coords()

    def place(half, bulk, other):
        if half == 0:
            return (y + bulk) % RING, (x + other) % RING
        return (y + other) % RING, (x + bulk) % RING

    def block(half, bulk, other, which, ref=rail):
        py, px = place(half, bulk, other)
        return part_of(ref, (py * RING + px) * PAD, half * hidden, which, hidden)

    def send(src, dst, key, half, axis, step):
        py, px = place(half, step, 0) if axis == 0 else place(half, 0, step)
        copies.start(src, dst, key, dp_index(py, px, core))

    def ways(other):
        return ((0, 1), (1, -1)) if other in (0, 3) else ((1, 1), (0, -1))

    def trim(ref, which):
        return part_of(ref, 0, 0, which, hidden)

    def narrow(ref, which):
        return ref.at[:, pl.ds(0, KEEP)] if which else ref

    def far(half, other):
        for which, step in ways(other):
            send(block(half, 2, other, which, rail_ref), narrow(near.at[half, other, which], which), ("n", half, other, which), half, 0, step)

    def pass_on(half, other):
        for which, step in ways(other):
            here = narrow(near.at[half, other, which], which)
            copies.wait_recv(here, ("n", half, other, which))
            ref = block(half, step, other, which)
            ref[...] = (ref[...].astype(F32) + here[...].astype(F32)).astype(BF16)
            side = 0 if step == 1 else 1
            for part in (0, 1):
                send(block(half, step, other, part), trim(whole.at[half, other, side], part), ("w", half, other, side, part), half, 0, step)

    def settle(half, other):
        for part in (0, 1):
            ref = block(half, 0, other, part)
            value = ref[...].astype(F32)
            for side in (0, 1):
                here = trim(whole.at[half, other, side], part)
                copies.wait_recv(here, ("w", half, other, side, part))
                value = value + here[...].astype(F32)
            ref[...] = value.astype(BF16)

    def far_last(half):
        for which, step in ways(0):
            send(block(half, 0, 2, which), narrow(near_last.at[half, which], which), ("nl", half, which), half, 1, step)

    def pass_last(half):
        for which, step in ways(0):
            here = narrow(near_last.at[half, which], which)
            copies.wait_recv(here, ("nl", half, which))
            ref = block(half, 0, step, which)
            ref[...] = (ref[...].astype(F32) + here[...].astype(F32)).astype(BF16)
            side = 0 if step == 1 else 1
            for part in (0, 1):
                send(block(half, 0, step, part), trim(whole_last.at[half, side], part), ("wl", half, side, part), half, 1, step)

    def total(half):
        sums = []
        for part in (0, 1):
            value = block(half, 0, 0, part)[...].astype(F32)
            for side in (0, 1):
                here = trim(whole_last.at[half, side], part)
                copies.wait_recv(here, ("wl", half, side, part))
                value = value + here[...].astype(F32)
            sums.append(value)
        return sums

    return far, pass_on, settle, far_last, pass_last, total


def update_kernel(
    rail_ref, back_ref, next_ref, gain_ref, mg_ref, mu_ref, og_ref, ou_ref, sg_ref, su_ref,
    result_ref, out_ref, nmg_ref, nmu_ref, nog_ref, nou_ref, nsg_ref, nsu_ref, scale_ref,
    weights, rail, near, whole, near_last, whole_last, spread, gather, next_pad, block_ref, flat_ref,
    state, updates, gate_sum, up_sum, send_sem, recv_sem, local_sem, state_sem,
):
    y, x, core = coords()
    hidden = out_ref.shape[1]
    features = next_ref.shape[1]
    copies = Copies(send_sem, recv_sem)
    fetch = pltpu.make_async_copy(rail_ref, rail, local_sem)
    fetch.start()
    loads = [
        pltpu.make_async_copy(ref.at[:, 0, :], state.at[i], state_sem.at[i])
        for i, ref in enumerate((mg_ref, mu_ref, og_ref, ou_ref, sg_ref, su_ref))
    ]
    for load in loads:
        load.start()
    plane_barrier()
    far, pass_on, settle, far_last, pass_last, total = reduce_steps(
        rail_ref, rail, near, whole, near_last, whole_last, copies, hidden
    )
    order = (2, 1, 3, 0)
    for other in order:
        far(0, other)
        far(1, other)
    fetch.wait()
    pad_matrix(spread, 1)
    widened, inverse = rms(next_ref[...])
    next_normed = (widened * inverse * gain_ref[...]).astype(BF16)
    next_pad[...] = mm(next_normed, spread[...]).astype(BF16)
    pad_matrix(gather, 0)
    result_ref[...] = mm(back_ref[...], gather[...]).astype(BF16)
    for other in order:
        pass_on(0, other)
        pass_on(1, other)
    for other in order:
        settle(0, other)
        settle(1, other)
        if other == 2:
            far_last(0)
            far_last(1)
    pass_last(0)
    pass_last(1)

    begin, rounds, from_sibling = gather_steps(weights, copies, hidden)
    lanes = flat_ref.shape[1]
    lines = hidden // lanes
    mine = pl.multiple_of(lax.axis_index("dp") * PAD, PAD)
    for load in loads:
        load.wait()
    stores = []
    for half, outs in ((0, (nmg_ref, nog_ref, nsg_ref)), (1, (nmu_ref, nou_ref, nsu_ref))):
        upper, lower = total(half)
        lower = jnp.concatenate([lower, last_columns(lower, hidden - KEEP)], axis=1)
        for line in range(lines):
            span = slice(line * lanes, (line + 1) * lanes)
            flat_ref[pl.ds(line, PAD // 2, stride=lines), :] = upper[:, span]
            flat_ref[pl.ds(PAD // 2 * lines + line, ROWS - PAD // 2, stride=lines), :] = lower[
                : ROWS - PAD // 2, span
            ]
        gradient = flat_ref[...]
        results = adam_update(state[half], state[2 + half], state[4 + half], gradient)
        for i, value in enumerate(results):
            number = 2 * i + half
            updates[number] = value
            stores.append(
                pltpu.make_async_copy(updates.at[number], outs[i].at[:, 0, :], state_sem.at[number])
            )
            stores[-1].start()
        updated = results[0]
        peak = jnp.max(jnp.abs(updated), keepdims=True)
        high = peak.astype(BF16).astype(F32)
        middle = (peak - high).astype(BF16).astype(F32)
        low = peak - high - middle
        tail = lax.broadcasted_iota(jnp.int32, (PAD - ROWS, hidden), 0)
        for line in range(lines):
            block_ref[pl.ds(0, ROWS), pl.ds(line * lanes, lanes)] = updates[half, pl.ds(line, ROWS, stride=lines), :]
        block_ref[pl.ds(ROWS, PAD - ROWS), :] = jnp.where(
            tail == 0, high, jnp.where(tail == 1, middle, jnp.where(tail == 2, low, 0.0))
        )
        pack(block_ref, 0, 0, hidden)
        weights[pl.ds(mine, PAD), pl.ds(half * hidden, hidden)] = block_ref[...].astype(BF16)
        begin(half)
    width = next_pad.shape[1] // RING

    def line_of(half, step, cols):
        rows = pl.ds(pl.multiple_of(((y + step) % RING) * width, width), width)
        return mm(next_pad[:, rows], weights[rows, pl.ds(half * hidden + cols.start, cols.size)])

    def line_ready(half, step):
        for i in range(RING):
            from_sibling(half, *((i, step) if half == 0 else (step, i)))
        for number in range(width // PAD):
            unpack(weights, ((y + step) % RING) * width + number * PAD, half * hidden, hidden)

    def add_line(half, step, target, fresh):
        line_ready(half, step)
        for piece in tiles(hidden):
            cols = pl.ds(*piece)
            product = line_of(half, step, cols)
            target[:, cols] = product if fresh else target[:, cols] + product

    after = {
        2: lambda: add_line(0, 0, gate_sum, True),
        4: lambda: add_line(1, 0, up_sum, True),
        6: lambda: add_line(1, 3, up_sum, False),
        8: lambda: add_line(1, 1, up_sum, False),
    }
    for number, items in enumerate(rounds):
        for item in items:
            item()
        if number in after:
            after[number]()
    for step in (3, 1, 2):
        line_ready(0, step)
    line_ready(1, 2)

    peaks = []
    for half in (0, 1):
        heads = weights[:, pl.ds(half * hidden + 3 * (hidden - KEEP), 128)].astype(F32)
        heads = heads.reshape(heads.shape[0] // PAD, PAD, 128)[:, PAD - 8 :, :]
        level = lax.broadcasted_iota(jnp.int32, heads.shape, 1)
        found = jnp.sum(jnp.where(level >= 4, heads, 0.0), axis=1)
        peaks.append(jnp.max(found, keepdims=True) + scale_eps)
    lane = lax.broadcasted_iota(jnp.int32, scale_ref.shape, 1)
    scale_ref[...] = jnp.where(lane == 0, peaks[0], peaks[1])
    for start, size in tiles(hidden):
        cols = pl.ds(start, size)
        gate = gate_sum[:, cols]
        for step in (3, 1, 2):
            gate = gate + line_of(0, step, cols)
        up = up_sum[:, cols] + line_of(1, 2, cols)
        out_ref[:, cols] = (gate / (1.0 + jnp.exp(-gate)) * up).astype(BF16)
    for store in stores:
        store.wait()
    copies.wait_sends()


def deliver_kernel(count, *refs):
    sources, targets = refs[:count], refs[count : 2 * count]
    holds, load_sem, store_sem = refs[2 * count : 3 * count - 1], refs[-2], refs[-1]

    def flat(ref):
        return ref.at[:, 0, :] if len(ref.shape) == 3 else ref

    loads = [
        pltpu.make_async_copy(flat(sources[i]), hold, load_sem.at[i]) for i, hold in enumerate(holds)
    ]
    stores = [
        pltpu.make_async_copy(hold, flat(targets[i]), store_sem.at[i]) for i, hold in enumerate(holds)
    ]
    for load in loads:
        load.start()
    targets[-1][...] = sources[-1][...]
    for load, store in zip(loads, stores):
        load.wait()
        store.start()
    for store in stores:
        store.wait()


VMEM = pl.BlockSpec(memory_space=pltpu.VMEM)
SMEM = pl.BlockSpec(memory_space=pltpu.SMEM)
ANY = pl.BlockSpec(memory_space=pl.ANY)
HBM = pl.BlockSpec(memory_space=pltpu.HBM)


def shards(
    section_inputs,
    cotangent,
    norm_gain,
    quant_gate,
    quant_up,
    scales,
    down_proj,
    master_gate,
    master_up,
    moment_gate,
    moment_up,
    second_gate,
    second_up,
    next_inputs,
):
    tokens, features = cotangent.shape
    hidden = quant_gate.shape[2]
    partners = lax.axis_size("dp")
    padded = partners * PAD
    rail_rows = padded // CORES
    dma = pltpu.SemaphoreType.DMA
    back, rail = pl.pallas_call(
        back_kernel,
        out_shape=(
            jax.ShapeDtypeStruct((tokens, padded), BF16),
            jax.ShapeDtypeStruct((rail_rows, 2 * hidden), BF16),
        ),
        in_specs=[VMEM, VMEM, VMEM, VMEM, VMEM, SMEM, ANY],
        out_specs=(VMEM, HBM),
        scratch_shapes=[
            pltpu.VMEM((padded, 2 * hidden), BF16),
            pltpu.VMEM((2 * hidden, padded), BF16),
            pltpu.VMEM((hidden, features), BF16),
            pltpu.VMEM((padded, hidden), BF16),
            pltpu.VMEM((features, padded), BF16),
            pltpu.VMEM((padded, features), BF16),
            pltpu.VMEM((tokens, padded), BF16),
            pltpu.VMEM((tokens, padded), F32),
            pltpu.VMEM((tokens, 1), F32),
            pltpu.VMEM((1, padded), F32),
            pltpu.VMEM((tokens, hidden), F32),
            pltpu.VMEM((tokens, hidden), F32),
            pltpu.VMEM((tokens, hidden), F32),
            pltpu.VMEM((max(PARTS), hidden), F32),
            pltpu.VMEM((tokens, padded), BF16),
            pltpu.VMEM((2 * tokens, 2 * hidden), BF16),
            pltpu.VMEM((rail_rows, 3 * tokens), BF16),
            pltpu.VMEM((PAD, 2 * hidden), BF16),
            pltpu.VMEM((rail_rows, 2 * hidden), BF16),
            dma((160,)),
            dma((160,)),
            dma((len(PARTS) * RING,)),
            dma((len(PARTS) * RING,)),
            dma(()),
            dma((2,)),
        ],
        compiler_params=pltpu.CompilerParams(
            collective_id=0, has_side_effects=True, vmem_limit_bytes=60 * 2**20
        ),
    )(quant_gate[0], quant_up[0], section_inputs[0], cotangent, norm_gain, scales, down_proj[0])
    lanes = 128
    lines = ROWS * hidden // lanes
    row = jax.ShapeDtypeStruct((lines, 1, lanes), F32)
    flat = [
        value.transpose(1, 0, 2).reshape(row.shape)
        for value in (master_gate, master_up, moment_gate, moment_up, second_gate, second_up)
    ]
    outs = pl.pallas_call(
        update_kernel,
        out_shape=(
            jax.ShapeDtypeStruct((tokens, features), BF16),
            jax.ShapeDtypeStruct((tokens, hidden), BF16),
        )
        + (row,) * 6
        + (jax.ShapeDtypeStruct((1, 2), F32),),
        in_specs=[HBM] + [VMEM] * 3 + [ANY] * 6,
        out_specs=(VMEM,) * 2 + (ANY,) * 6 + (VMEM,),
        scratch_shapes=[
            pltpu.VMEM((padded, 2 * hidden), BF16),
            pltpu.VMEM((rail_rows, 2 * hidden), BF16),
            pltpu.VMEM((2, RING, 2, PAD // 2, hidden), BF16),
            pltpu.VMEM((2, RING, 2, PAD, hidden), BF16),
            pltpu.VMEM((2, 2, PAD // 2, hidden), BF16),
            pltpu.VMEM((2, 2, PAD, hidden), BF16),
            pltpu.VMEM((features, padded), BF16),
            pltpu.VMEM((padded, features), BF16),
            pltpu.VMEM((tokens, padded), BF16),
            pltpu.VMEM((PAD, hidden), F32),
            pltpu.VMEM((lines, lanes), F32),
            pltpu.VMEM((6, lines, lanes), F32),
            pltpu.VMEM((6, lines, lanes), F32),
            pltpu.VMEM((tokens, hidden), F32),
            pltpu.VMEM((tokens, hidden), F32),
            dma((200,)),
            dma((200,)),
            dma(()),
            dma((6,)),
        ],
        compiler_params=pltpu.CompilerParams(
            collective_id=1, has_side_effects=True, vmem_limit_bytes=60 * 2**20
        ),
    )(rail, back, next_inputs[0], norm_gain, *flat)
    outs = pl.pallas_call(
        functools.partial(deliver_kernel, len(outs)),
        out_shape=tuple(jax.ShapeDtypeStruct(value.shape, value.dtype) for value in outs),
        in_specs=[HBM] * 8 + [VMEM],
        out_specs=(HBM,) * 8 + (VMEM,),
        scratch_shapes=[
            pltpu.VMEM((value.shape[0], value.shape[-1]), value.dtype) for value in outs[:-1]
        ]
        + [dma((8,)), dma((8,))],
        compiler_params=pltpu.CompilerParams(vmem_limit_bytes=60 * 2**20),
    )(*outs)
    result, next_hidden = outs[:2]
    return (
        (result[None],)
        + tuple(value.reshape(ROWS, 1, hidden).transpose(1, 0, 2) for value in outs[2:8])
        + (outs[8], next_hidden[None])
    )


def solution(mesh):
    placed = (
        P("section", "dp", None),
        P("dp", None),
        P("section", None),
        P("section", "dp", None),
        P("section", "dp", None),
        P("section", None),
        P("section", None, None),
        P("section", "dp", None),
        P("section", "dp", None),
        P("section", "dp", None),
        P("section", "dp", None),
        P("section", "dp", None),
        P("section", "dp", None),
        P("section", "dp", None),
    )
    return jax.shard_map(
        shards,
        mesh=mesh,
        in_specs=placed,
        out_specs=(
            P("section", "dp", None),
            P("section", "dp", None),
            P("section", "dp", None),
            P("section", "dp", None),
            P("section", "dp", None),
            P("section", "dp", None),
            P("section", "dp", None),
            P("section", None),
            P("section", "dp", None),
        ),
        check_vma=False,
    )
```
